32 devices in a mesh: groups: 2 (over x), dev: 16 (over z, y, core).
Axes of the slice: x: 2, y: 2, z: 4, core: 2. Of those that a mesh axis runs over, the one named last changes fastest.
Arguments:
- queries: bfloat16 [2, 32, 128, 1024], P(None, ('groups', 'dev')), parts along dimension 1, may hold values from -180 to 180
- keys_values: bfloat16 [2, 32, 2, 1664, 128], P(None, ('groups', 'dev')), parts along dimension 1, may hold values from -6 to 6
- residual: bfloat16 [2, 2048, 2048], P(None, ('groups', 'dev')), parts along dimension 1, may hold values from -6 to 6
- norm_gain: float32 [2048], replicated, may hold values from 0.1 to 1.9
- gate_up: bfloat16 [16, 2048, 1536], P('dev'), may hold values from -0.125 to 0.125
- down_proj: bfloat16 [16, 768, 2048], P('dev'), may hold values from -0.21875 to 0.21875
- expert_ids: int32 [2, 2048, 8], P(None, ('groups', 'dev')), parts along dimension 1, may hold values from 0 to 15, all different within a row; in each aligned block of 64 rows (0 to 63, 64 to 127, ..., all dimensions but the last counted through in order) at most 40 rows name the same one
- expert_gates: int32 [2, 2048, 8], P(None, ('groups', 'dev')), parts along dimension 1, may hold values from 1 to 1023
Outputs:
- layer_out: bfloat16 [2, 2048, 2048], P(None, ('groups', 'dev')), parts along dimension 1
The draws below stay inside these ranges and needn't reach their ends.
There are 2 independent parts, one for each index of `groups`. The reference program is written for one: setup_inputs(seed, part) draws one part's arguments, and reference() takes and returns one part's arrays. A program takes and returns all parts, laid end to end along the dimension named above; an argument that names none is the same for every part. Nothing has to cross between parts.
Inputs may be any that keep to these rules, and one draw needn't show every extreme that they name: `expert_ids`: in each micro-batch and each aligned block of 64 rows (the tokens of one device), no expert is named by more than 40 rows, a bound that some block reaches; the 8 experts of a row differ.
All inputs are finite; a program needn't handle non-finite values.
Results may differ from the reference program's by a relative error of at most 0.0039.
Values may be sent and summed in bfloat16 or wider, within the bound.
A program may use at most 128 MiB of HBM per device.

```python
import math
import jax
import jax.numpy as jnp
import numpy as np
from jax import lax

D = 2048
FF = 768
HD = 128
GQ = 8
KVH = 2
TOPK = 8
MB = 2
SPAN = 128
SEQS = 8
UNITS = 16
CTX = 1664
TOK_DEV = 64
TOKENS = 1024
EXPERTS = 16
CAP = 40
N_DEV = 16


def joint_draw(key):
    seed_pairs = jax.random.fold_in(key, 101)
    seed_query = jax.random.fold_in(key, 202)
    cached_pairs = jnp.clip(jax.random.normal(seed_pairs, (MB, UNITS, 2, CTX, HD), jnp.float32), -6.0, 6.0)
    query_rows = jnp.clip(2.0 * jax.random.normal(seed_query, (MB, UNITS, SPAN, GQ * HD), jnp.float32), -12.0, 12.0)
    return (cached_pairs, query_rows)


def draw_queries(key, part):
    return joint_draw(key)[1].astype(jnp.bfloat16)


def draw_keys_values(key, part):
    return joint_draw(key)[0].astype(jnp.bfloat16)


def plant(result, key, smallest, top_value):
    longest = result.shape.index(max(result.shape))
    spots = []
    for shift in (0, 1):
        where = [jax.random.randint(jax.random.fold_in(key, axis), (), 0, length) for axis, length in enumerate(result.shape)]
        where[longest] = (where[longest] + shift) % result.shape[longest]
        spots.append(tuple(where))
    return result.at[spots[0]].set(smallest).at[spots[1]].set(top_value)


def block_levels(key, dims, cuts, smallest, high):
    level, own = 1.0, jax.random.fold_in(key, 6)
    for axis_at, parts in cuts:
        draws = jnp.exp(jax.random.uniform(jax.random.fold_in(own, axis_at), (parts,), jnp.float32, smallest / len(cuts), high / len(cuts)))
        level = level * jnp.repeat(draws, dims[axis_at] // parts).reshape([-1 if axis == axis_at else 1 for axis in range(len(dims))])
    return level


def routed_block(key, own, number, rows, number_of, top, most, skew):
    order = jax.random.permutation(key, number_of)
    crowded, ordinary = load_shares(number_of, rows * top, most, skew, True), load_shares(number_of, rows * top, most, skew, False)
    places = jnp.arange(number_of)

    def named(lengths, offset_by):
        used = int((lengths > 0).sum())
        fixed = max(1, used // 4)
        shifted = fixed + (places - fixed + offset_by * (used - fixed)) % max(1, number_of - fixed)
        return jnp.zeros((number_of,), jnp.int32).at[order[jnp.where(places < fixed, places, shifted)]].set(jnp.asarray(lengths, jnp.int32))

    lengths = jnp.where(number % 4 == 0, named(crowded, number // 4), named(ordinary, number - number // 4 - 1))
    mixed = jax.random.permutation(jax.random.fold_in(own, 3), number_of)
    giver, receiver = mixed[0:number_of // 2 * 2:2], mixed[1:number_of // 2 * 2:2]
    slack = jnp.minimum(lengths[giver] - 1, most - lengths[receiver]) // 2
    slack = jnp.where((giver == order[0]) | (receiver == order[0]) | (lengths[receiver] == 0), 0, jnp.maximum(slack, 0))
    shifted = jax.random.randint(jax.random.fold_in(own, 4), (number_of // 2,), 0, 1 << 20) % (slack + 1)
    lengths = lengths.at[giver].add(-shifted).at[receiver].add(shifted)
    labels = jnp.searchsorted(jnp.cumsum(lengths), jnp.arange(rows * top), side="right").astype(jnp.int32)
    table = labels.reshape(top, rows).T
    table = table[jax.random.permutation(jax.random.fold_in(own, 1), rows)]
    offset_by = jax.random.randint(jax.random.fold_in(own, 2), (rows, 1), 0, top)
    return jnp.take_along_axis(table, (jnp.arange(top)[None, :] + offset_by) % top, axis=1)


def load_shares(number_of, total, most, slope, full):
    portions = [(1 << 20) // math.isqrt(rank ** slope) + 1 for rank in range(1, number_of + 1)]
    largest = most if full else min(most, max(-(-total // number_of), total * portions[0] // sum(portions)))
    least = 1 if total - largest >= number_of - 1 else 0
    counts, spare = [largest] + [least] * (number_of - 1), total - largest - least * (number_of - 1)
    while spare > 0:
        free = [i for i in range(1, number_of) if counts[i] < largest] or [i for i in range(1, number_of) if counts[i] < most]
        whole, remaining = sum([portions[i] for i in free]), spare
        for i in free:
            extra = min(most - counts[i], max(1, remaining * portions[i] // whole), spare)
            counts[i] = counts[i] + extra
            spare = spare - extra
    return np.array(counts)


def centred(stream_key, extent, width, limit, shards=(), kind=jnp.bfloat16):
    values = width * jax.random.normal(stream_key, extent, jnp.float32)
    if shards:
        values = values * block_levels(stream_key, extent, shards, -0.22, 0.18)
    return jnp.clip(values, -limit, limit).astype(kind)


def setup_inputs(seed: int = 0, part: int = 0) -> dict:
    streams_of = jax.random.split(jax.random.key(seed), 9)
    part_splits = jax.random.split(jax.random.fold_in(streams_of[8], part), 9)
    queries = draw_queries(jax.random.fold_in(jax.random.fold_in(streams_of[8], part), 71), part)
    keys_values = draw_keys_values(jax.random.fold_in(jax.random.fold_in(streams_of[8], part), 71), part)
    residual = centred(part_splits[2], (MB, TOKENS, D), 1.0, 6.0, ((1, 16),))
    norm_gain = jnp.clip(1.0 + 0.18 * jax.random.normal(streams_of[3], (D,), jnp.float32), 0.1, 1.9)
    gate_up = centred(streams_of[4], (EXPERTS, D, 2 * FF), D ** -0.5, 0.125, ((0, 16),))
    down_proj = centred(streams_of[5], (EXPERTS, FF, D), FF ** -0.5, 0.21875, ((0, 16),))
    expert_ids_keys = jax.random.split(jax.random.fold_in(part_splits[6], 1), MB * TOKENS // TOK_DEV)
    expert_ids_turns = jax.random.permutation(jax.random.fold_in(part_splits[6], 3), MB * TOKENS // TOK_DEV)
    expert_ids = jax.vmap(lambda own, number: routed_block(jax.random.fold_in(part_splits[6], 2), own, number, TOK_DEV, EXPERTS, TOPK, CAP, 1))(expert_ids_keys, expert_ids_turns).reshape((MB, TOKENS, TOPK))
    expert_gates = plant(jax.random.randint(part_splits[7], (MB, TOKENS, TOPK), 1, 1024), jax.random.fold_in(part_splits[7], 1), 1, 1023).astype(jnp.int32)
    return {"queries": queries, "keys_values": keys_values, "residual": residual, "norm_gain": norm_gain, "gate_up": gate_up, "down_proj": down_proj, "expert_ids": expert_ids, "expert_gates": expert_gates}


def attend(query_rows, cached_pairs):
    batches, length, feat_width = query_rows.shape
    context = cached_pairs.shape[2]
    head_size = cached_pairs.shape[3]
    groups = feat_width // head_size
    head_rows = query_rows.reshape(batches, length, groups, head_size).astype(jnp.float32)
    scores = jnp.einsum('mqgd,mkd->mgqk', head_rows, cached_pairs[:, 0].astype(jnp.float32)) / math.sqrt(head_size)
    query_pos = context - length + lax.broadcasted_iota(jnp.int32, (length, context), 0)
    key_pos = lax.broadcasted_iota(jnp.int32, (length, context), 1)
    allowed = key_pos <= query_pos
    scores = jnp.where(allowed, scores, -1e+30)
    highest = lax.optimization_barrier(jnp.max(scores, axis=-1, keepdims=True))
    scaled_exp = jnp.where(allowed, jnp.exp(scores - highest), 0.0)
    totals = lax.optimization_barrier(jnp.sum(scaled_exp, axis=-1, keepdims=True))
    weights = (scaled_exp / totals).astype(jnp.bfloat16)
    blended = jnp.einsum('mgqk,mkd->mqgd', weights.astype(jnp.float32), cached_pairs[:, 1].astype(jnp.float32))
    return blended.astype(jnp.bfloat16).reshape(batches, length, feat_width)

def reference(queries, keys_values, residual, norm_gain, gate_up, down_proj, expert_ids, expert_gates):
    unit_first = (jnp.moveaxis(queries, 1, 0), jnp.moveaxis(keys_values, 1, 0))
    blended_heads = lax.map(lambda unit_pair: attend(unit_pair[0], unit_pair[1]), unit_first)
    grouped = blended_heads.reshape(SEQS, KVH, MB, N_DEV, SPAN // N_DEV, GQ * HD)
    attn_rows = jnp.transpose(grouped, (2, 3, 0, 4, 1, 5)).reshape(MB, TOKENS, D)
    stream = residual.astype(jnp.float32) + attn_rows.astype(jnp.float32)
    meansq = lax.optimization_barrier(jnp.mean(stream * stream, axis=-1, keepdims=True))
    normed = (stream * lax.rsqrt(meansq + 1e-06) * norm_gain).astype(jnp.bfloat16)
    shares = expert_gates.astype(jnp.float32)
    shares = shares / lax.optimization_barrier(jnp.sum(shares, axis=-1, keepdims=True))
    flat_ids = expert_ids.reshape(MB, N_DEV, TOK_DEV * TOPK)
    one_hot = (flat_ids[..., None] == jnp.arange(EXPERTS, dtype=jnp.int32)).astype(jnp.int32)
    ranking = lax.optimization_barrier(jnp.sum((jnp.cumsum(one_hot, axis=2) - one_hot) * one_hot, axis=-1)).astype(jnp.int32)
    batch_ids = lax.broadcasted_iota(jnp.int32, flat_ids.shape, 0)
    source_ids = lax.broadcasted_iota(jnp.int32, flat_ids.shape, 1)
    entry_ids = lax.broadcasted_iota(jnp.int32, flat_ids.shape, 2)
    token_rows = (batch_ids * TOKENS + source_ids * TOK_DEV + entry_ids // TOPK).astype(jnp.int32)
    row_table = jnp.zeros((EXPERTS, MB, N_DEV, CAP), jnp.int32).at[flat_ids, batch_ids, source_ids, ranking].set(token_rows)
    share_table = jnp.zeros((EXPERTS, MB, N_DEV, CAP), jnp.float32).at[flat_ids, batch_ids, source_ids, ranking].set(shares.reshape(MB, N_DEV, TOK_DEV * TOPK))
    flat_normed = normed.reshape(MB * TOKENS, D)

    def expert_turn(running, inputs):
        row_ids, share_ids, gate_mat, down_mat = inputs
        index_list = row_ids.reshape(-1)
        rows_in = flat_normed[index_list]
        projected = jnp.dot(rows_in, gate_mat, preferred_element_type=jnp.float32)
        hidden = (jax.nn.silu(projected[:, :FF]) * projected[:, FF:]).astype(jnp.bfloat16)
        output = jnp.dot(hidden, down_mat, preferred_element_type=jnp.float32).astype(jnp.bfloat16)
        running = running.at[index_list].add(share_ids.reshape(-1, 1) * output.astype(jnp.float32))
        return (running, None)
    start_sum = jnp.zeros((MB * TOKENS, D), jnp.float32)
    mixture, ignored = lax.scan(expert_turn, start_sum, (row_table, share_table, gate_up, down_proj))
    return (stream + mixture.reshape(MB, TOKENS, D)).astype(jnp.bfloat16)
```

```python
import functools
import math

import jax
import jax.numpy as jnp
from jax import lax
from jax.experimental import pallas as pl
from jax.experimental.pallas import tpu as pltpu
from jax.sharding import PartitionSpec as P


def attend_pair(heads, pair_rows, keys, values):
    length = pair_rows.shape[0]
    context, head_size = keys.shape
    past = context - length
    query = jnp.concatenate(
        [pair_rows[:, head * head_size : (head + 1) * head_size] for head in range(heads)], axis=0
    )
    scores = lax.dot_general(
        query, keys, (((1,), (1,)), ((), ())), preferred_element_type=jnp.float32
    )
    scores = scores * (1.0 / math.sqrt(head_size))
    old, new = scores[:, :past], scores[:, past:]
    row = lax.broadcasted_iota(jnp.int32, new.shape, 0) % length
    col = lax.broadcasted_iota(jnp.int32, new.shape, 1)
    allowed = col <= row
    new = jnp.where(allowed, new, -1e30)
    highest = jnp.maximum(
        jnp.max(old, axis=-1, keepdims=True), jnp.max(new, axis=-1, keepdims=True)
    )
    old = jnp.exp(old - highest)
    new = jnp.where(allowed, jnp.exp(new - highest), 0.0)
    totals = jnp.sum(old, axis=-1, keepdims=True) + jnp.sum(new, axis=-1, keepdims=True)
    share = 1.0 / totals
    blended = jnp.dot(
        (old * share).astype(jnp.bfloat16), values[:past],
        preferred_element_type=jnp.float32,
    ) + jnp.dot(
        (new * share).astype(jnp.bfloat16), values[past:],
        preferred_element_type=jnp.float32,
    )
    return blended


def attend_kernel(heads, q_ref, kv_ref, out_ref):
    length = q_ref.shape[1]
    head_size = kv_ref.shape[4]
    blended = attend_pair(heads, q_ref[0], kv_ref[0, 0, 0], kv_ref[0, 0, 1])
    for head in range(heads):
        out_ref[0, :, head * head_size : (head + 1) * head_size] = blended[
            head * length : (head + 1) * length
        ].astype(jnp.bfloat16)


def attend_local(queries, keys_values):
    batches, unit, length, feat_width = queries.shape
    context, head_size = keys_values.shape[3:]
    heads = 2
    wide = heads * head_size
    return pl.pallas_call(
        functools.partial(attend_kernel, heads),
        grid=(batches, feat_width // wide),
        out_shape=jax.ShapeDtypeStruct((batches, length, feat_width), jnp.bfloat16),
        in_specs=[
            pl.BlockSpec((1, length, wide), lambda b, h: (b, 0, h)),
            pl.BlockSpec((1, 1, 2, context, head_size), lambda b, h: (b, 0, 0, 0, 0)),
        ],
        out_specs=pl.BlockSpec((1, length, wide), lambda b, h: (b, 0, h)),
        compiler_params=pltpu.CompilerParams(vmem_limit_bytes=40 * 1024 * 1024),
    )(queries.reshape(batches, length, feat_width), keys_values)


def to_owners(exchanged, kv_heads):
    batches, sources, positions, feat_width = exchanged.shape
    grouped = exchanged.reshape(batches, sources // kv_heads, kv_heads, positions, feat_width)
    grouped = jnp.transpose(grouped, (0, 1, 3, 2, 4))
    return grouped.reshape(batches, sources // kv_heads * positions, kv_heads * feat_width)


def prepare(attn_rows, residual, norm_gain):
    stream = residual.astype(jnp.float32) + attn_rows.astype(jnp.float32)
    meansq = jnp.mean(stream * stream, axis=-1, keepdims=True)
    normed = (stream * lax.rsqrt(meansq + 1e-06) * norm_gain).astype(jnp.bfloat16)
    return stream, normed


def dense_shares(expert_ids, expert_gates, experts):
    shares = expert_gates.astype(jnp.float32)
    shares = shares / jnp.sum(shares, axis=-1, keepdims=True)
    named = expert_ids[..., None] == jnp.arange(experts, dtype=jnp.int32)
    return jnp.sum(jnp.where(named, shares[..., None], 0.0), axis=-2)


def run_expert(rows_in, gate_up, down_proj, weight):
    hidden_width = down_proj.shape[1]
    projected = jnp.dot(rows_in, gate_up[0], preferred_element_type=jnp.float32)
    hidden = (jax.nn.silu(projected[:, :hidden_width]) * projected[:, hidden_width:]).astype(
        jnp.bfloat16
    )
    output = jnp.dot(hidden, down_proj[0], preferred_element_type=jnp.float32)
    return (output * weight).astype(jnp.bfloat16)


MESH = pl.DeviceIdType.MESH


def moe_kernel(
    q_ref, kv_ref, res_ref, gain_ref, ids_ref, gates_ref, gu_hbm, dn_hbm, out_ref,
    heads_ref, attn, stream, gathered, partial, pairbuf, sumbuf, gu, dn, xs, act, share_out, share_in,
    load_sem, sh_send, sh_recv, ex_send, ex_recv, ag_send, ag_recv, agp_send, agp_recv,
    rsp_send, rsp_recv, rs_send, rs_recv,
):
    chunks, chips, _, rows, width = gathered.shape
    batches = q_ref.shape[0]
    per = chunks // batches
    devices = 2 * chips
    seqs, kv_heads, span, part = attn.shape[1:]
    hidden = dn.shape[0]
    depth = chips // 2
    me = lax.axis_index("dev")
    core = me % 2
    mine = me // 2
    y = mine % 2
    z = mine // 2
    half = z // (depth // 2)
    inner = ((z + 1) // 2) % 2 == 1
    outer = ((z + 1) // 2) % 2 == 0

    def pair(level):
        return 2 * level + y, 2 * level + 1 - y

    same, cross = pair(z)
    twin, twin_x = pair(z + 1 - 2 * (z % 2))
    near, near_x = pair(2 - half)
    far, far_x = pair((depth - 1) * (1 - half))
    over_y, over_t, over_n = cross * 2 + core, twin * 2 + core, near * 2 + core
    partner = mine * 2 + 1 - core

    def remote(src, dst, send, recv, target):
        return pltpu.make_async_remote_copy(
            src_ref=src, dst_ref=dst, send_sem=send, recv_sem=recv,
            device_id={"dev": target}, device_id_type=MESH,
        )

    def gather(k, origin, index, target):
        slot = gathered.at[k, origin, core]
        return remote(slot, slot, ag_send.at[k, index], ag_recv.at[k, origin], target)

    def gathered_from(k, origin):
        return gather(k, origin, 0, over_y)

    def pair_copy(k, origin):
        slot = gathered.at[k, origin, core]
        return remote(slot, slot, agp_send.at[k, origin], agp_recv.at[k, origin], partner)

    def pair_arrival(k, origin):
        slot = gathered.at[k, origin, 1 - core]
        return remote(slot, slot, agp_send.at[k, origin], agp_recv.at[k, origin], partner)

    def sum_copy(k, dest):
        return remote(
            partial.at[k, dest, 1 - core], pairbuf.at[k, dest],
            rsp_send.at[k, dest], rsp_recv.at[k, dest], partner,
        )

    def reduce(k, dest, slot, target):
        return remote(
            partial.at[k, dest, core], sumbuf.at[k, slot],
            rs_send.at[k, dest], rs_recv.at[k, slot], target,
        )

    def arrived(k, slot):
        reduce(k, same, slot, over_y).wait_recv()
        return sumbuf[k, slot].astype(jnp.float32)

    def exchange(batch, target):
        return remote(
            heads_ref.at[batch, target], attn.at[batch, me // kv_heads, me % kv_heads],
            ex_send.at[batch, target], ex_recv.at[batch, me], target,
        )

    def arrival(batch, source):
        slot = attn.at[batch, source // kv_heads, source % kv_heads]
        return remote(slot, slot, ex_send.at[batch, source], ex_recv.at[batch, source], source)

    def share_copy(target):
        return remote(
            share_out.at[target], share_in.at[me], sh_send.at[target], sh_recv.at[me], target
        )

    def share_arrival(source):
        slot = share_in.at[source]
        return remote(slot, slot, sh_send.at[source], sh_recv.at[source], source)

    loads = (
        pltpu.make_async_copy(gu_hbm.at[0], gu, load_sem.at[0]),
        pltpu.make_async_copy(dn_hbm.at[0], dn, load_sem.at[1]),
    )
    for load in loads:
        load.start()

    barrier = pltpu.get_barrier_semaphore()

    @pl.loop(1, devices)
    def _(k):
        target = (me + k) % devices
        pl.semaphore_signal(barrier, inc=1, device_id={"dev": target}, device_id_type=MESH)

    ids = jnp.concatenate([ids_ref[batch] for batch in range(batches)], axis=1)
    gates = jnp.concatenate([gates_ref[batch] for batch in range(batches)], axis=1)
    gates = gates.astype(jnp.float32)
    gates = gates / jnp.sum(gates, axis=0, keepdims=True)
    for expert in range(devices):
        share_out[expert] = jnp.sum(jnp.where(ids == expert, gates, 0.0), axis=0, keepdims=True)
    share_in[me] = share_out[me]

    head_size = kv_ref.shape[3]

    def attend(batch):
        @pl.loop(0, part // (2 * head_size))
        def _(h):
            cols = pl.ds(pl.multiple_of(h * 2 * head_size, 2 * head_size), 2 * head_size)
            blended = attend_pair(2, q_ref[batch, :, cols], kv_ref[batch, 0], kv_ref[batch, 1])
            length = q_ref.shape[1]
            for head in range(2):
                at = pl.ds(pl.multiple_of((h * 2 + head) * head_size, head_size), head_size)
                piece = blended[head * length : (head + 1) * length]
                heads_ref[batch, :, :, at] = piece.reshape(
                    devices, length // devices, head_size
                ).astype(jnp.bfloat16)

    def send_heads(batch):
        @pl.loop(1, devices)
        def _(k):
            exchange(batch, (me + k) % devices).start()

    def take_heads(batch):
        attn[batch, me // kv_heads, me % kv_heads] = heads_ref[batch, me]

        @pl.loop(1, devices)
        def _(k):
            arrival(batch, (me + k) % devices).wait_recv()

        some = seqs // per
        for at in range(per):
            chunk = batch * per + at
            squares = jnp.zeros((rows, 1), jnp.float32)
            for head in range(kv_heads):
                cols = slice(head * part, (head + 1) * part)
                added = attn[batch, at * some : (at + 1) * some, head].astype(jnp.float32)
                added = added.reshape(rows, part) + res_ref[chunk, :, cols].astype(jnp.float32)
                stream[chunk, :, cols] = added
                squares = squares + jnp.sum(added * added, axis=-1, keepdims=True)
            scale = lax.rsqrt(squares / width + 1e-06)
            gathered[chunk, same, core] = (stream[chunk] * scale * gain_ref[...]).astype(
                jnp.bfloat16
            )

    def send_own(k):
        gather(k, same, 0, over_y).start()
        gather(k, same, 1, over_t).start()

        @pl.when(inner)
        def _():
            gather(k, same, 2, over_n).start()

        pair_copy(k, same).start()

    def compute(k, places):
        blocks = [(place, which) for place in places for which in range(2)]
        for place in places:
            pair_arrival(k, place).wait_recv()
        weights = []
        for at, (place, which) in enumerate(blocks):
            xs[at * rows : (at + 1) * rows, :] = gathered[k, place, which]
            spread = jnp.broadcast_to(share_in[place * 2 + which], (rows, share_in.shape[2]))
            lane = lax.broadcasted_iota(jnp.int32, spread.shape, 1)
            row = lax.broadcasted_iota(jnp.int32, spread.shape, 0)
            mine_only = jnp.where(lane == row + k * rows, spread, 0.0)
            weights.append(jnp.sum(mine_only, axis=-1, keepdims=True))
        weight = jnp.concatenate(weights, axis=0)
        gate = jnp.dot(xs[...], gu[:, :hidden], preferred_element_type=jnp.float32)
        up = jnp.dot(xs[...], gu[:, hidden:], preferred_element_type=jnp.float32)
        act[...] = (gate / (1.0 + jnp.exp(-gate)) * up).astype(jnp.bfloat16)
        tile = 512
        for col in range(0, width, tile):
            result = jnp.dot(
                act[...], dn[:, col : col + tile], preferred_element_type=jnp.float32
            ) * weight
            for at, (place, which) in enumerate(blocks):
                partial[k, place, which, :, col : col + tile] = result[
                    at * rows : (at + 1) * rows
                ].astype(jnp.bfloat16)
        for place in places:
            sum_copy(k, place).start()

    def both(k, dest):
        sum_copy(k, dest).wait_recv()
        return partial[k, dest, core].astype(jnp.float32) + pairbuf[k, dest].astype(jnp.float32)

    def put(k, dest, total):
        partial[k, dest, core] = total.astype(jnp.bfloat16)

    def finish(k):
        total = stream[k] + both(k, same) + arrived(k, 3) + arrived(k, 8)

        @pl.when(inner)
        def _():
            out_ref[k] = (total + arrived(k, 7)).astype(out_ref.dtype)

        @pl.when(outer)
        def _():
            out_ref[k] = total.astype(out_ref.dtype)

    attend(0)
    pl.semaphore_wait(barrier, devices - 1)

    @pl.loop(1, devices)
    def _(k):
        share_copy((me + k) % devices).start()

    send_heads(0)
    for batch in range(1, batches):
        attend(batch)
    take_heads(0)
    send_own(0)
    for batch in range(1, batches):
        send_heads(batch)

    @pl.loop(1, devices)
    def _(k):
        share_arrival((me + k) % devices).wait_recv()

    for load in loads:
        load.wait()

    @pl.loop(0, chunks + 1)
    def _(k):
        gathers = k < chunks
        reduces = k > 0
        j = k - 1

        @pl.when(reduces)
        def _():
            for dest, slot, target in ((far_x, 0, over_y), (twin_x, 2, over_t), (near_x, 1, over_y)):
                put(j, dest, both(j, dest))
                reduce(j, dest, slot, target).start()

        @pl.when(gathers)
        def _():
            gathered_from(k, cross).wait_recv()

            @pl.when(outer)
            def _():
                gather(k, cross, 3, over_t).start()

            pair_copy(k, cross).start()
            compute(k, (same, cross))

        @pl.when(reduces)
        def _():
            @pl.when(outer)
            def _():
                put(j, far, both(j, far) + arrived(j, 0))
                reduce(j, far, 4, over_t).start()

            @pl.when(inner)
            def _():
                put(j, far, both(j, far) + arrived(j, 0) + arrived(j, 4))
                reduce(j, far, 5, over_n).start()

        @pl.when(gathers)
        def _():
            gathered_from(k, twin).wait_recv()

            @pl.when(inner)
            def _():
                gather(k, twin, 4, over_n).start()

            pair_copy(k, twin).start()
            gathered_from(k, near).wait_recv()
            gather(k, near, 5, over_y).start()

            @pl.when(inner)
            def _():
                gather(k, near, 6, over_t).start()

            pair_copy(k, near).start()
            compute(k, (twin, near))

        @pl.when(reduces)
        def _():
            put(j, cross, both(j, cross) + arrived(j, 2))
            reduce(j, cross, 3, over_y).start()

            @pl.when(outer)
            def _():
                put(j, near, both(j, near) + arrived(j, 1))
                reduce(j, near, 6, over_t).start()

            @pl.when(inner)
            def _():
                put(j, near, both(j, near) + arrived(j, 1) + arrived(j, 6))
                reduce(j, near, 7, over_n).start()

        @pl.when(gathers)
        def _():
            gathered_from(k, far).wait_recv()
            gather(k, far, 7, over_y).start()

            @pl.when(inner)
            def _():
                gather(k, far, 8, over_t).start()
                gather(k, cross, 3, over_t).start()

            pair_copy(k, far).start()
            gathered_from(k, near_x).wait_recv()
            pair_copy(k, near_x).start()
            compute(k, (far, near_x))

        for batch in range(1, batches):

            @pl.when(k + 1 == batch * per)
            def _():
                take_heads(batch)

        @pl.when(k + 1 < chunks)
        def _():
            send_own(k + 1)

        @pl.when(reduces)
        def _():
            @pl.when(outer)
            def _():
                put(j, twin, both(j, twin))

            @pl.when(inner)
            def _():
                put(j, twin, both(j, twin) + arrived(j, 5))

            reduce(j, twin, 8, over_t).start()

        @pl.when(gathers)
        def _():
            gathered_from(k, twin_x).wait_recv()
            pair_copy(k, twin_x).start()
            gathered_from(k, far_x).wait_recv()
            pair_copy(k, far_x).start()
            compute(k, (twin_x, far_x))

        @pl.when(k > 1)
        def _():
            finish(k - 2)

    finish(chunks - 1)

    @pl.loop(1, devices)
    def _(k):
        share_copy((me + k) % devices).wait_send()
        for batch in range(batches):
            exchange(batch, (me + k) % devices).wait_send()

    @pl.loop(0, chunks)
    def _(k):
        for index in (0, 1, 3, 5, 7):
            gather(k, same, index, over_y).wait_send()

        @pl.when(inner)
        def _():
            for index in (2, 4, 6, 8):
                gather(k, same, index, over_y).wait_send()

        for dest in (cross, twin, twin_x, near, near_x, far, far_x):
            reduce(k, dest, 0, over_y).wait_send()

        @pl.loop(0, chips)
        def _(chip):
            pair_copy(k, chip).wait_send()
            sum_copy(k, chip).wait_send()


def chunk_rows(rows, span):
    return max(rows // 2, 2 * span)


def fits(devices, batches, rows, width, hidden, span):
    tokens = batches * rows
    piece = chunk_rows(rows, span)
    block = tokens * width * 2
    needed = block * (5 * devices // 2 + 9) + 3 * width * hidden * 2 + 8 * block
    regular = rows % piece == 0 and piece % 16 == 0 and piece % span == 0 and tokens % 128 == 0
    return devices == 2 * 2 * 4 and regular and needed < 48 * 1024 * 1024


def routed_layer(queries, keys_values, residual, norm_gain, ids, gates, gate_up, down_proj, kv_heads, devices):
    batches, rows, width = residual.shape
    length, part = queries.shape[1:]
    span = length // devices
    hidden = down_proj.shape[1]
    chips = devices // 2
    piece = chunk_rows(rows, span)
    chunks = batches * rows // piece
    dma = pltpu.SemaphoreType.DMA
    vmem = pl.BlockSpec(memory_space=pltpu.VMEM)
    anywhere = pl.BlockSpec(memory_space=pl.ANY)
    kind = jnp.bfloat16
    out = pl.pallas_call(
        moe_kernel,
        out_shape=jax.ShapeDtypeStruct((chunks, piece, width), kind),
        in_specs=[vmem] * 6 + [anywhere] * 2,
        out_specs=vmem,
        scratch_shapes=[
            pltpu.VMEM((batches, devices, span, part), kind),
            pltpu.VMEM((batches, devices // kv_heads, kv_heads, span, part), kind),
            pltpu.VMEM((chunks, piece, width), jnp.float32),
            pltpu.VMEM((chunks, chips, 2, piece, width), kind),
            pltpu.VMEM((chunks, chips, 2, piece, width), kind),
            pltpu.VMEM((chunks, chips, piece, width), kind),
            pltpu.VMEM((chunks, 9, piece, width), kind),
            pltpu.VMEM((width, 2 * hidden), kind),
            pltpu.VMEM((hidden, width), kind),
            pltpu.VMEM((4 * piece, width), kind),
            pltpu.VMEM((4 * piece, hidden), kind),
            pltpu.VMEM((devices, 1, batches * rows), jnp.float32),
            pltpu.VMEM((devices, 1, batches * rows), jnp.float32),
            dma((2,)),
            dma((devices,)), dma((devices,)),
            dma((batches, devices)), dma((batches, devices)),
            dma((chunks, 9)), dma((chunks, chips)),
            dma((chunks, chips)), dma((chunks, chips)),
            dma((chunks, chips)), dma((chunks, chips)),
            dma((chunks, chips)), dma((chunks, 9)),
        ],
        compiler_params=pltpu.CompilerParams(
            collective_id=0, has_side_effects=True, vmem_limit_bytes=56 * 1024 * 1024
        ),
    )(
        queries, keys_values, residual.reshape(chunks, piece, width), norm_gain.reshape(1, width),
        jnp.transpose(ids, (0, 2, 1)), jnp.transpose(gates, (0, 2, 1)), gate_up, down_proj,
    )
    return out.reshape(batches, rows, width)


def body(queries, keys_values, residual, norm_gain, gate_up, down_proj, expert_ids, expert_gates):
    devices = lax.axis_size("dev")
    me = lax.axis_index("dev")
    model_width = residual.shape[2]
    kv_heads = model_width // queries.shape[3]
    experts = devices * gate_up.shape[0]
    batches, unit, length, feat_width = queries.shape
    positions = length // devices
    if gate_up.shape[0] == 1 and unit == 1 and length % devices == 0 and fits(
        devices, batches, residual.shape[1], model_width, down_proj.shape[1], positions
    ):
        return routed_layer(
            queries[:, 0], keys_values[:, 0], residual, norm_gain, expert_ids, expert_gates,
            gate_up, down_proj, kv_heads, devices,
        )
    weights = dense_shares(expert_ids, expert_gates, experts)
    blended = attend_local(queries, keys_values)
    weights = lax.all_gather(weights, "dev", axis=1, tiled=True)
    mine = jnp.sum(
        jnp.where(jnp.arange(experts, dtype=jnp.int32) == me, weights, 0.0), axis=-1, keepdims=True
    )
    pieces = []
    for batch_index in range(batches):
        outgoing_rows = blended[batch_index].reshape(1, devices, positions, feat_width)
        arrived_rows = lax.all_to_all(outgoing_rows, "dev", split_axis=1, concat_axis=1, tiled=True)
        attn_rows = to_owners(arrived_rows, kv_heads)
        stream, normed = prepare(attn_rows[0], residual[batch_index], norm_gain)
        rows_in = lax.all_gather(normed, "dev", axis=0, tiled=True)
        partial = run_expert(rows_in, gate_up, down_proj, mine[batch_index])
        summed = lax.psum_scatter(partial, "dev", scatter_dimension=0, tiled=True)
        pieces.append((stream + summed.astype(jnp.float32)).astype(jnp.bfloat16))
    return jnp.stack(pieces, axis=0)


def solution(mesh):
    in_specs = (
        P(None, ("groups", "dev"), None, None),
        P(None, ("groups", "dev"), None, None, None),
        P(None, ("groups", "dev"), None),
        P(),
        P("dev", None, None),
        P("dev", None, None),
        P(None, ("groups", "dev"), None),
        P(None, ("groups", "dev"), None),
    )
    out_specs = P(None, ("groups", "dev"), None)
    return jax.shard_map(body, mesh=mesh, in_specs=in_specs, out_specs=out_specs, check_vma=False)
```

```python
import functools
import math

import jax
import jax.numpy as jnp
from jax import lax
from jax.experimental import pallas as pl
from jax.experimental.pallas import tpu as pltpu
from jax.sharding import PartitionSpec as P


def attend_pair(heads, pair_rows, keys, values):
    length = pair_rows.shape[0]
    context, head_size = keys.shape
    past = context - length
    query = jnp.concatenate(
        [pair_rows[:, head * head_size : (head + 1) * head_size] for head in range(heads)], axis=0
    )
    scores = lax.dot_general(
        query, keys, (((1,), (1,)), ((), ())), preferred_element_type=jnp.float32
    )
    scores = scores * (1.0 / math.sqrt(head_size))
    old, new = scores[:, :past], scores[:, past:]
    row = lax.broadcasted_iota(jnp.int32, new.shape, 0) % length
    col = lax.broadcasted_iota(jnp.int32, new.shape, 1)
    allowed = col <= row
    new = jnp.where(allowed, new, -1e30)
    highest = jnp.maximum(
        jnp.max(old, axis=-1, keepdims=True), jnp.max(new, axis=-1, keepdims=True)
    )
    old = jnp.exp(old - highest)
    new = jnp.where(allowed, jnp.exp(new - highest), 0.0)
    totals = jnp.sum(old, axis=-1, keepdims=True) + jnp.sum(new, axis=-1, keepdims=True)
    share = 1.0 / totals
    blended = jnp.dot(
        (old * share).astype(jnp.bfloat16), values[:past],
        preferred_element_type=jnp.float32,
    ) + jnp.dot(
        (new * share).astype(jnp.bfloat16), values[past:],
        preferred_element_type=jnp.float32,
    )
    return blended


def attend_kernel(heads, q_ref, kv_ref, out_ref):
    length = q_ref.shape[1]
    head_size = kv_ref.shape[4]
    blended = attend_pair(heads, q_ref[0], kv_ref[0, 0, 0], kv_ref[0, 0, 1])
    for head in range(heads):
        out_ref[0, :, head * head_size : (head + 1) * head_size] = blended[
            head * length : (head + 1) * length
        ].astype(jnp.bfloat16)


def attend_local(queries, keys_values):
    batches, unit, length, feat_width = queries.shape
    context, head_size = keys_values.shape[3:]
    heads = 2
    wide = heads * head_size
    return pl.pallas_call(
        functools.partial(attend_kernel, heads),
        grid=(batches, feat_width // wide),
        out_shape=jax.ShapeDtypeStruct((batches, length, feat_width), jnp.bfloat16),
        in_specs=[
            pl.BlockSpec((1, length, wide), lambda b, h: (b, 0, h)),
            pl.BlockSpec((1, 1, 2, context, head_size), lambda b, h: (b, 0, 0, 0, 0)),
        ],
        out_specs=pl.BlockSpec((1, length, wide), lambda b, h: (b, 0, h)),
        compiler_params=pltpu.CompilerParams(vmem_limit_bytes=40 * 1024 * 1024),
    )(queries.reshape(batches, length, feat_width), keys_values)


def to_owners(exchanged, kv_heads):
    batches, sources, positions, feat_width = exchanged.shape
    grouped = exchanged.reshape(batches, sources // kv_heads, kv_heads, positions, feat_width)
    grouped = jnp.transpose(grouped, (0, 1, 3, 2, 4))
    return grouped.reshape(batches, sources // kv_heads * positions, kv_heads * feat_width)


def prepare(attn_rows, residual, norm_gain):
    stream = residual.astype(jnp.float32) + attn_rows.astype(jnp.float32)
    meansq = jnp.mean(stream * stream, axis=-1, keepdims=True)
    normed = (stream * lax.rsqrt(meansq + 1e-06) * norm_gain).astype(jnp.bfloat16)
    return stream, normed


def dense_shares(expert_ids, expert_gates, experts):
    shares = expert_gates.astype(jnp.float32)
    shares = shares / jnp.sum(shares, axis=-1, keepdims=True)
    named = expert_ids[..., None] == jnp.arange(experts, dtype=jnp.int32)
    return jnp.sum(jnp.where(named, shares[..., None], 0.0), axis=-2)


def run_expert(rows_in, gate_up, down_proj, weight):
    hidden_width = down_proj.shape[1]
    projected = jnp.dot(rows_in, gate_up[0], preferred_element_type=jnp.float32)
    hidden = (jax.nn.silu(projected[:, :hidden_width]) * projected[:, hidden_width:]).astype(
        jnp.bfloat16
    )
    output = jnp.dot(hidden, down_proj[0], preferred_element_type=jnp.float32)
    return (output * weight).astype(jnp.bfloat16)


MESH = pl.DeviceIdType.MESH


def moe_kernel(
    chips, q_ref, kv_ref, res_ref, gain_ref, ids_ref, gates_ref, gu_hbm, dn_hbm, out_ref,
    heads_ref, attn, stream, gathered, partial, pairbuf, ringbuf, gu, dn, xs, sh, act, share_out, share_in,
    load_sem, sh_send, sh_recv, ex_send, ex_recv, ag_send, ag_recv, agp_send, agp_recv, rsp_send, rsp_recv, rs_send, rs_recv,
):
    batches, rows, width = res_ref.shape
    devices = 2 * chips
    kv_heads, part = attn.shape[2], attn.shape[4]
    hidden = dn.shape[0]
    far = chips // 2
    me = lax.axis_index("dev")
    core = me % 2
    mine = me // 2
    odd = mine % 2
    pos = odd * ((mine + 1) // 2) + (1 - odd) * ((chips - mine // 2) % chips)

    def chip_at(place):
        q = (place + 2 * chips) % chips
        upper = q // (far + 1)
        some = (q + chips - 1) // chips
        return some * ((1 - upper) * (2 * q - 1) + upper * 2 * (chips - q))

    partner = mine * 2 + (1 - core)
    ahead = (chip_at(pos + 1) * 2 + core, chip_at(pos - 1) * 2 + core)
    sign = (1, -1)

    def remote(src, dst, send, recv, target):
        return pltpu.make_async_remote_copy(
            src_ref=src, dst_ref=dst, send_sem=send, recv_sem=recv,
            device_id={"dev": target}, device_id_type=MESH,
        )

    def ag_copy(way, dist, batch, origin):
        slot = gathered.at[batch, origin, core]
        return remote(
            slot, slot,
            ag_send.at[way, dist - 1, batch], ag_recv.at[way, dist - 1, batch], ahead[way],
        )

    def pair_copy(batch, origin):
        slot = gathered.at[batch, origin, core]
        return remote(slot, slot, agp_send.at[batch, origin], agp_recv.at[batch, origin], partner)

    def pair_arrival(batch, origin):
        slot = gathered.at[batch, origin, 1 - core]
        return remote(slot, slot, agp_send.at[batch, origin], agp_recv.at[batch, origin], partner)

    def sum_copy(batch, dest):
        return remote(
            partial.at[batch, dest, 1 - core], pairbuf.at[batch, dest],
            rsp_send.at[batch, dest], rsp_recv.at[batch, dest], partner,
        )

    def rs_copy(way, turn, batch, dest):
        return remote(
            partial.at[batch, dest, core], ringbuf.at[way, turn, batch],
            rs_send.at[way, turn, batch], rs_recv.at[way, turn, batch], ahead[way],
        )

    def exchange(batch, target, cols=slice(None)):
        return remote(
            heads_ref.at[batch, target, :, cols],
            attn.at[batch, me // kv_heads, me % kv_heads, :, cols],
            ex_send.at[batch, target], ex_recv.at[batch, me], target,
        )

    def share_copy(target):
        return remote(
            share_out.at[target], share_in.at[me], sh_send.at[target], sh_recv.at[me], target
        )

    def share_arrival(source):
        slot = share_in.at[source]
        return remote(slot, slot, sh_send.at[source], sh_recv.at[source], source)

    def arrival(batch, source):
        slot = attn.at[batch, source // kv_heads, source % kv_heads]
        return remote(slot, slot, ex_send.at[batch, source], ex_recv.at[batch, source], source)

    loads = (
        pltpu.make_async_copy(gu_hbm.at[0], gu, load_sem.at[0]),
        pltpu.make_async_copy(dn_hbm.at[0], dn, load_sem.at[1]),
    )
    for load in loads:
        load.start()

    barrier = pltpu.get_barrier_semaphore()

    @pl.loop(1, devices)
    def _(k):
        target = (me + k) % devices
        pl.semaphore_signal(barrier, inc=1, device_id={"dev": target}, device_id_type=MESH)

    ids = jnp.concatenate([ids_ref[batch] for batch in range(batches)], axis=1)
    gates = jnp.concatenate([gates_ref[batch] for batch in range(batches)], axis=1)
    gates = gates.astype(jnp.float32)
    gates = gates / jnp.sum(gates, axis=0, keepdims=True)
    for expert in range(devices):
        share_out[expert] = jnp.sum(jnp.where(ids == expert, gates, 0.0), axis=0, keepdims=True)
    share_in[me] = share_out[me]

    head_size = kv_ref.shape[3]
    length = q_ref.shape[1]
    pieces = 2

    def attend(batch, piece):
        each = part // (2 * head_size) // pieces

        @pl.loop(piece * each, (piece + 1) * each)
        def _(h):
            cols = pl.ds(pl.multiple_of(h * 2 * head_size, 2 * head_size), 2 * head_size)
            blended = attend_pair(2, q_ref[batch, :, cols], kv_ref[batch, 0], kv_ref[batch, 1])
            for head in range(2):
                at = pl.ds(pl.multiple_of((h * 2 + head) * head_size, head_size), head_size)
                heads_ref[batch, :, :, at] = blended[head * length : (head + 1) * length].reshape(
                    devices, length // devices, head_size
                ).astype(jnp.bfloat16)

    def send_heads(batch, piece):
        cols = slice(piece * part // pieces, (piece + 1) * part // pieces)

        @pl.loop(1, devices)
        def _(k):
            exchange(batch, (me + k) % devices, cols).start()

    def take_heads(batch):
        attn[batch, me // kv_heads, me % kv_heads] = heads_ref[batch, me]

        @pl.loop(1, devices)
        def _(k):
            arrival(batch, (me + k) % devices).wait_recv()

        squares = jnp.zeros((rows, 1), jnp.float32)
        for head in range(kv_heads):
            cols = slice(head * part, (head + 1) * part)
            added = attn[batch, :, head].astype(jnp.float32).reshape(rows, part)
            added = added + res_ref[batch, :, cols].astype(jnp.float32)
            stream[batch, :, cols] = added
            squares = squares + jnp.sum(added * added, axis=-1, keepdims=True)
        scale = lax.rsqrt(squares / width + 1e-06)
        gathered[batch, mine, core] = (stream[batch] * scale * gain_ref[...]).astype(jnp.bfloat16)
        for way in range(2):
            ag_copy(way, 1, batch, mine).start()
        pair_copy(batch, mine).start()

    attend(0, 0)
    pl.semaphore_wait(barrier, devices - 1)
    send_heads(0, 0)
    attend(0, 1)
    send_heads(0, 1)

    @pl.loop(1, devices)
    def _(k):
        share_copy((me + k) % devices).start()

    attend(1, 0)
    send_heads(1, 0)
    take_heads(0)
    attend(1, 1)
    send_heads(1, 1)
    take_heads(1)

    @pl.loop(1, devices)
    def _(k):
        share_arrival((me + k) % devices).wait_recv()

    for load in loads:
        load.wait()

    tile = 512

    def compute(blocks):
        for at, (batch, chip, which) in enumerate(blocks):
            xs[at * rows : (at + 1) * rows, :] = gathered[batch, chip, which]
            spread = jnp.broadcast_to(share_in[chip * 2 + which], (rows, share_in.shape[2]))
            lane = lax.broadcasted_iota(jnp.int32, spread.shape, 1)
            row = lax.broadcasted_iota(jnp.int32, spread.shape, 0)
            share = jnp.sum(
                jnp.where(lane == row + batch * rows, spread, 0.0), axis=-1, keepdims=True
            )
            sh[at * rows : (at + 1) * rows, :] = jnp.broadcast_to(share, spread.shape)
        gate = jnp.dot(xs[...], gu[:, :hidden], preferred_element_type=jnp.float32)
        up = jnp.dot(xs[...], gu[:, hidden:], preferred_element_type=jnp.float32)
        act[...] = (gate / (1.0 + jnp.exp(-gate)) * up).astype(jnp.bfloat16)

        @pl.loop(0, width // tile)
        def _(j):
            cols = pl.ds(pl.multiple_of(j * tile, tile), tile)
            result = jnp.dot(act[...], dn[:, cols], preferred_element_type=jnp.float32)
            for at, (batch, chip, which) in enumerate(blocks):
                share = sh[at * rows : (at + 1) * rows, :1]
                piece = result[at * rows : (at + 1) * rows]
                partial[batch, chip, which, :, cols] = (piece * share).astype(jnp.bfloat16)

    for batch in range(batches):
        pair_arrival(batch, mine).wait_recv()
    compute([(batch, mine, which) for batch in range(batches) for which in range(2)])
    for batch in range(batches):
        sum_copy(batch, mine).start()

    @pl.loop(0, 2 * (far - 1))
    def _(step):
        dist = step // 2 + 1
        batch = step % 2
        origins = (chip_at(pos - dist), chip_at(pos + dist))
        for way in range(2):
            ag_copy(way, dist, batch, origins[way]).wait_recv()

            @pl.when((dist + 1 < far) | (batch == way))
            def _():
                ag_copy(way, dist + 1, batch, origins[way]).start()

            pair_copy(batch, origins[way]).start()
        for way in range(2):
            pair_arrival(batch, origins[way]).wait_recv()
        compute([(batch, origins[way], which) for way in range(2) for which in range(2)])
        for way in range(2):
            sum_copy(batch, origins[way]).start()

    def gather_sum(batch, dest):
        return partial[batch, dest, core].astype(jnp.float32) + pairbuf[batch, dest].astype(
            jnp.float32
        )

    for way in range(2):
        dest = chip_at(pos + sign[way] * (far - 1))
        batch = 1 - way
        sum_copy(batch, dest).wait_recv()
        partial[batch, dest, core] = gather_sum(batch, dest).astype(jnp.bfloat16)
        rs_copy(way, 1, batch, dest).start()

    last = chip_at(pos + far)
    for batch in range(batches):
        ag_copy(batch, far, batch, last).wait_recv()
        pair_copy(batch, last).start()
    for batch in range(batches):
        pair_arrival(batch, last).wait_recv()
    compute([(batch, last, which) for batch in range(batches) for which in range(2)])
    for batch in range(batches):
        sum_copy(batch, last).start()

    for batch in range(batches):
        sum_copy(batch, last).wait_recv()
        partial[batch, last, core] = gather_sum(batch, last).astype(jnp.bfloat16)
        rs_copy(batch, 0, batch, last).start()

    for way in range(2):
        dest = chip_at(pos + sign[way] * (far - 1))
        batch = way
        sum_copy(batch, dest).wait_recv()
        rs_copy(way, 0, batch, dest).wait_recv()
        partial[batch, dest, core] = (
            gather_sum(batch, dest) + ringbuf[way, 0, batch].astype(jnp.float32)
        ).astype(jnp.bfloat16)
        rs_copy(way, 1, batch, dest).start()

    @pl.loop(0, 2 * (far - 2))
    def _(step):
        turn = step // 2 + 2
        for way in range(2):
            batch = (step + 1 + way) % 2
            dest = chip_at(pos + sign[way] * (far - turn))
            sum_copy(batch, dest).wait_recv()
            rs_copy(way, turn - 1, batch, dest).wait_recv()
            partial[batch, dest, core] = (
                gather_sum(batch, dest) + ringbuf[way, turn - 1, batch].astype(jnp.float32)
            ).astype(jnp.bfloat16)
            rs_copy(way, turn, batch, dest).start()

    for batch in range(batches):
        sum_copy(batch, mine).wait_recv()
    for way in range(2):
        rs_copy(way, far - 1, 1 - way, mine).wait_recv()
    for way in range(2):
        rs_copy(way, far - 1, way, mine).wait_recv()
    for batch in range(batches):
        out_ref[batch] = (
            stream[batch]
            + (
                gather_sum(batch, mine)
                + ringbuf[0, far - 1, batch].astype(jnp.float32)
                + ringbuf[1, far - 1, batch].astype(jnp.float32)
            )
        ).astype(out_ref.dtype)

    @pl.loop(1, devices)
    def _(k):
        share_copy((me + k) % devices).wait_send()
        for batch in range(batches):
            exchange(batch, (me + k) % devices).wait_send()

    for way in range(2):
        for batch in range(batches):
            ag_copy(way, 1, batch, mine).wait_send()
        ag_copy(way, far, way, mine).wait_send()

        @pl.loop(0, 2 * (far - 2))
        def _(step):
            ag_copy(way, step // 2 + 2, step % 2, mine).wait_send()

        rs_copy(way, 0, way, mine).wait_send()

        @pl.loop(0, 2 * (far - 1))
        def _(step):
            rs_copy(way, step // 2 + 1, step % 2, mine).wait_send()

    @pl.loop(0, 2 * chips)
    def _(step):
        pair_copy(step % 2, step // 2).wait_send()
        sum_copy(step % 2, step // 2).wait_send()


def fits(devices, rows, width, hidden):
    block = 2 * rows * (width + 128) * 2
    needed = 3 * devices * block + 3 * width * hidden * 2 + 8 * rows * width * 4
    return devices % 4 == 0 and 8 <= devices <= 64 and 2 * rows % 128 == 0 and needed < 48 * 1024 * 1024


def routed_layer(queries, keys_values, residual, norm_gain, ids, gates, gate_up, down_proj, kv_heads, devices):
    batches, rows, width = residual.shape
    length, part = queries.shape[1:]
    span = length // devices
    hidden = down_proj.shape[1]
    chips = devices // 2
    far = chips // 2
    dma = pltpu.SemaphoreType.DMA
    vmem = pl.BlockSpec(memory_space=pltpu.VMEM)
    anywhere = pl.BlockSpec(memory_space=pl.ANY)
    kind = jnp.bfloat16
    return pl.pallas_call(
        functools.partial(moe_kernel, chips),
        out_shape=jax.ShapeDtypeStruct((batches, rows, width), kind),
        in_specs=[vmem] * 6 + [anywhere] * 2,
        out_specs=vmem,
        scratch_shapes=[
            pltpu.VMEM((batches, devices, span, part), kind),
            pltpu.VMEM((batches, devices // kv_heads, kv_heads, span, part), kind),
            pltpu.VMEM((batches, rows, width), jnp.float32),
            pltpu.VMEM((batches, chips, 2, rows, width), kind),
            pltpu.VMEM((batches, chips, 2, rows, width), kind),
            pltpu.VMEM((batches, chips, rows, width), kind),
            pltpu.VMEM((2, far, batches, rows, width), kind),
            pltpu.VMEM((width, 2 * hidden), kind),
            pltpu.VMEM((hidden, width), kind),
            pltpu.VMEM((4 * rows, width), kind),
            pltpu.VMEM((4 * rows, batches * rows), jnp.float32),
            pltpu.VMEM((4 * rows, hidden), kind),
            pltpu.VMEM((devices, 1, batches * rows), jnp.float32),
            pltpu.VMEM((devices, 1, batches * rows), jnp.float32),
            dma((2,)),
            dma((devices,)), dma((devices,)),
            dma((batches, devices)), dma((batches, devices)),
            dma((2, far, batches)), dma((2, far, batches)),
            dma((batches, chips)), dma((batches, chips)),
            dma((batches, chips)), dma((batches, chips)),
            dma((2, far, batches)), dma((2, far, batches)),
        ],
        compiler_params=pltpu.CompilerParams(
            collective_id=0, has_side_effects=True, vmem_limit_bytes=56 * 1024 * 1024
        ),
    )(
        queries, keys_values, residual, norm_gain.reshape(1, width),
        jnp.transpose(ids, (0, 2, 1)), jnp.transpose(gates, (0, 2, 1)), gate_up, down_proj,
    )


def body(queries, keys_values, residual, norm_gain, gate_up, down_proj, expert_ids, expert_gates):
    devices = lax.axis_size("dev")
    me = lax.axis_index("dev")
    model_width = residual.shape[2]
    kv_heads = model_width // queries.shape[3]
    experts = devices * gate_up.shape[0]
    batches, unit, length, feat_width = queries.shape
    positions = length // devices
    if batches == 2 and fits(devices, residual.shape[1], model_width, down_proj.shape[1]):
        return routed_layer(
            queries[:, 0], keys_values[:, 0], residual, norm_gain, expert_ids, expert_gates,
            gate_up, down_proj, kv_heads, devices,
        )
    weights = dense_shares(expert_ids, expert_gates, experts)
    blended = attend_local(queries, keys_values)
    weights = lax.all_gather(weights, "dev", axis=1, tiled=True)
    mine = jnp.sum(
        jnp.where(jnp.arange(experts, dtype=jnp.int32) == me, weights, 0.0), axis=-1, keepdims=True
    )
    pieces = []
    for batch_index in range(batches):
        outgoing_rows = blended[batch_index].reshape(1, devices, positions, feat_width)
        arrived_rows = lax.all_to_all(outgoing_rows, "dev", split_axis=1, concat_axis=1, tiled=True)
        attn_rows = to_owners(arrived_rows, kv_heads)
        stream, normed = prepare(attn_rows[0], residual[batch_index], norm_gain)
        rows_in = lax.all_gather(normed, "dev", axis=0, tiled=True)
        partial = run_expert(rows_in, gate_up, down_proj, mine[batch_index])
        summed = lax.psum_scatter(partial, "dev", scatter_dimension=0, tiled=True)
        pieces.append((stream + summed.astype(jnp.float32)).astype(jnp.bfloat16))
    return jnp.stack(pieces, axis=0)


def solution(mesh):
    in_specs = (
        P(None, ("groups", "dev"), None, None),
        P(None, ("groups", "dev"), None, None, None),
        P(None, ("groups", "dev"), None),
        P(),
        P("dev", None, None),
        P("dev", None, None),
        P(None, ("groups", "dev"), None),
        P(None, ("groups", "dev"), None),
    )
    out_specs = P(None, ("groups", "dev"), None)
    return jax.shard_map(body, mesh=mesh, in_specs=in_specs, out_specs=out_specs, check_vma=False)
```

```python
import functools
import math

import jax
import jax.numpy as jnp
from jax import lax
from jax.experimental import pallas as pl
from jax.experimental.pallas import tpu as pltpu
from jax.sharding import PartitionSpec as P


def attend_pair(heads, pair_rows, keys, values):
    length = pair_rows.shape[0]
    context, head_size = keys.shape
    past = context - length
    query = jnp.concatenate(
        [pair_rows[:, head * head_size : (head + 1) * head_size] for head in range(heads)], axis=0
    )
    scores = lax.dot_general(
        query, keys, (((1,), (1,)), ((), ())), preferred_element_type=jnp.float32
    )
    scores = scores * (1.0 / math.sqrt(head_size))
    old, new = scores[:, :past], scores[:, past:]
    row = lax.broadcasted_iota(jnp.int32, new.shape, 0) % length
    col = lax.broadcasted_iota(jnp.int32, new.shape, 1)
    allowed = col <= row
    new = jnp.where(allowed, new, -1e30)
    highest = jnp.maximum(
        jnp.max(old, axis=-1, keepdims=True), jnp.max(new, axis=-1, keepdims=True)
    )
    old = jnp.exp(old - highest)
    new = jnp.where(allowed, jnp.exp(new - highest), 0.0)
    totals = jnp.sum(old, axis=-1, keepdims=True) + jnp.sum(new, axis=-1, keepdims=True)
    share = 1.0 / totals
    blended = jnp.dot(
        (old * share).astype(jnp.bfloat16), values[:past],
        preferred_element_type=jnp.float32,
    ) + jnp.dot(
        (new * share).astype(jnp.bfloat16), values[past:],
        preferred_element_type=jnp.float32,
    )
    return blended


def attend_kernel(heads, q_ref, kv_ref, out_ref):
    length = q_ref.shape[1]
    head_size = kv_ref.shape[4]
    blended = attend_pair(heads, q_ref[0], kv_ref[0, 0, 0], kv_ref[0, 0, 1])
    for head in range(heads):
        out_ref[0, :, head * head_size : (head + 1) * head_size] = blended[
            head * length : (head + 1) * length
        ].astype(jnp.bfloat16)


def attend_local(queries, keys_values):
    batches, unit, length, feat_width = queries.shape
    context, head_size = keys_values.shape[3:]
    heads = 2
    wide = heads * head_size
    return pl.pallas_call(
        functools.partial(attend_kernel, heads),
        grid=(batches, feat_width // wide),
        out_shape=jax.ShapeDtypeStruct((batches, length, feat_width), jnp.bfloat16),
        in_specs=[
            pl.BlockSpec((1, length, wide), lambda b, h: (b, 0, h)),
            pl.BlockSpec((1, 1, 2, context, head_size), lambda b, h: (b, 0, 0, 0, 0)),
        ],
        out_specs=pl.BlockSpec((1, length, wide), lambda b, h: (b, 0, h)),
        compiler_params=pltpu.CompilerParams(vmem_limit_bytes=40 * 1024 * 1024),
    )(queries.reshape(batches, length, feat_width), keys_values)


def to_owners(exchanged, kv_heads):
    batches, sources, positions, feat_width = exchanged.shape
    grouped = exchanged.reshape(batches, sources // kv_heads, kv_heads, positions, feat_width)
    grouped = jnp.transpose(grouped, (0, 1, 3, 2, 4))
    return grouped.reshape(batches, sources // kv_heads * positions, kv_heads * feat_width)


def prepare(attn_rows, residual, norm_gain):
    stream = residual.astype(jnp.float32) + attn_rows.astype(jnp.float32)
    meansq = jnp.mean(stream * stream, axis=-1, keepdims=True)
    normed = (stream * lax.rsqrt(meansq + 1e-06) * norm_gain).astype(jnp.bfloat16)
    return stream, normed


def dense_shares(expert_ids, expert_gates, experts):
    shares = expert_gates.astype(jnp.float32)
    shares = shares / jnp.sum(shares, axis=-1, keepdims=True)
    named = expert_ids[..., None] == jnp.arange(experts, dtype=jnp.int32)
    return jnp.sum(jnp.where(named, shares[..., None], 0.0), axis=-2)


def run_expert(rows_in, gate_up, down_proj, weight):
    hidden_width = down_proj.shape[1]
    projected = jnp.dot(rows_in, gate_up[0], preferred_element_type=jnp.float32)
    hidden = (jax.nn.silu(projected[:, :hidden_width]) * projected[:, hidden_width:]).astype(
        jnp.bfloat16
    )
    output = jnp.dot(hidden, down_proj[0], preferred_element_type=jnp.float32)
    return (output * weight).astype(jnp.bfloat16)


MESH = pl.DeviceIdType.MESH


def moe_kernel(
    chips, q_hbm, kv_hbm, res_hbm, gain_hbm, ids_hbm, gates_hbm, gu_hbm, dn_hbm, out_ref,
    q_ref, kv_ref, res_ref, gain_ref, ids_ref, gates_ref,
    heads_ref, attn, stream, gathered, partial, pairbuf, ringbuf, gu, dn, xs, sh, act, share_out, share_in,
    load_sem, sh_send, sh_recv, ex_send, ex_recv, ag_send, ag_recv, agp_send, agp_recv, rsp_send, rsp_recv, rs_send, rs_recv,
):
    batches, rows, width = res_ref.shape
    devices = 2 * chips
    kv_heads, part = attn.shape[2], attn.shape[4]
    hidden = dn.shape[0]
    far = chips // 2
    me = lax.axis_index("dev")
    core = me % 2
    mine = me // 2
    odd = mine % 2
    pos = odd * ((mine + 1) // 2) + (1 - odd) * ((chips - mine // 2) % chips)

    def chip_at(place):
        q = (place + 2 * chips) % chips
        upper = q // (far + 1)
        some = (q + chips - 1) // chips
        return some * ((1 - upper) * (2 * q - 1) + upper * 2 * (chips - q))

    partner = mine * 2 + (1 - core)
    ahead = (chip_at(pos + 1) * 2 + core, chip_at(pos - 1) * 2 + core)
    sign = (1, -1)

    def remote(src, dst, send, recv, target):
        return pltpu.make_async_remote_copy(
            src_ref=src, dst_ref=dst, send_sem=send, recv_sem=recv,
            device_id={"dev": target}, device_id_type=MESH,
        )

    def ag_copy(way, dist, batch, origin):
        slot = gathered.at[batch, origin, core]
        return remote(
            slot, slot,
            ag_send.at[way, dist - 1, batch], ag_recv.at[way, dist - 1, batch], ahead[way],
        )

    def pair_copy(batch, origin):
        slot = gathered.at[batch, origin, core]
        return remote(slot, slot, agp_send.at[batch, origin], agp_recv.at[batch, origin], partner)

    def pair_arrival(batch, origin):
        slot = gathered.at[batch, origin, 1 - core]
        return remote(slot, slot, agp_send.at[batch, origin], agp_recv.at[batch, origin], partner)

    def sum_copy(batch, dest):
        return remote(
            partial.at[batch, dest, 1 - core], pairbuf.at[batch, dest],
            rsp_send.at[batch, dest], rsp_recv.at[batch, dest], partner,
        )

    def rs_copy(way, turn, batch, dest):
        return remote(
            partial.at[batch, dest, core], ringbuf.at[way, turn, batch],
            rs_send.at[way, turn, batch], rs_recv.at[way, turn, batch], ahead[way],
        )

    def exchange(batch, target, cols=slice(None)):
        return remote(
            heads_ref.at[batch, target, :, cols],
            attn.at[batch, me // kv_heads, me % kv_heads, :, cols],
            ex_send.at[batch, target], ex_recv.at[batch, me], target,
        )

    def share_copy(target):
        return remote(
            share_out.at[target], share_in.at[me], sh_send.at[target], sh_recv.at[me], target
        )

    def share_arrival(source):
        slot = share_in.at[source]
        return remote(slot, slot, sh_send.at[source], sh_recv.at[source], source)

    def arrival(batch, source):
        slot = attn.at[batch, source // kv_heads, source % kv_heads]
        return remote(slot, slot, ex_send.at[batch, source], ex_recv.at[batch, source], source)

    barrier = pltpu.get_barrier_semaphore()

    @pl.loop(1, devices)
    def _(k):
        target = (me + k) % devices
        pl.semaphore_signal(barrier, inc=1, device_id={"dev": target}, device_id_type=MESH)

    pairs = [(q_hbm.at[0], q_ref.at[0]), (kv_hbm.at[0], kv_ref.at[0])]
    pairs += [(ids_hbm, ids_ref), (gates_hbm, gates_ref), (gain_hbm, gain_ref), (res_hbm, res_ref)]
    for batch in range(1, batches):
        pairs += [(q_hbm.at[batch], q_ref.at[batch]), (kv_hbm.at[batch], kv_ref.at[batch])]
    pairs += [(gu_hbm.at[0], gu), (dn_hbm.at[0], dn)]
    loads = [
        pltpu.make_async_copy(src, dst, load_sem.at[at]) for at, (src, dst) in enumerate(pairs)
    ]
    for load in loads:
        load.start()

    head_size = kv_ref.shape[3]
    length = q_ref.shape[1]

    wide = 2 * head_size
    pieces = part // wide

    def columns(piece):
        return pl.ds(pl.multiple_of(piece * wide, wide), wide)

    def attend(batch, piece):
        cols = columns(piece)
        blended = attend_pair(2, q_ref[batch, :, cols], kv_ref[batch, 0], kv_ref[batch, 1])
        for head in range(2):
            at = pl.ds(pl.multiple_of(piece * wide + head * head_size, head_size), head_size)
            heads_ref[batch, :, :, at] = blended[head * length : (head + 1) * length].reshape(
                devices, length // devices, head_size
            ).astype(jnp.bfloat16)

    def send_heads(batch, piece):
        cols = columns(piece)

        @pl.loop(1, devices)
        def _(k):
            exchange(batch, (me + k) % devices, cols).start()

    def take_heads(batch):
        attn[batch, me // kv_heads, me % kv_heads] = heads_ref[batch, me]

        @pl.loop(1, devices)
        def _(k):
            arrival(batch, (me + k) % devices).wait_recv()

        squares = jnp.zeros((rows, 1), jnp.float32)
        for head in range(kv_heads):
            cols = slice(head * part, (head + 1) * part)
            added = attn[batch, :, head].astype(jnp.float32).reshape(rows, part)
            added = added + res_ref[batch, :, cols].astype(jnp.float32)
            stream[batch, :, cols] = added
            squares = squares + jnp.sum(added * added, axis=-1, keepdims=True)
        scale = lax.rsqrt(squares / width + 1e-06)
        gathered[batch, mine, core] = (stream[batch] * scale * gain_ref[...]).astype(jnp.bfloat16)
        for way in range(2):
            ag_copy(way, 1, batch, mine).start()
        pair_copy(batch, mine).start()

    for load in loads[:2]:
        load.wait()
    attend(0, 0)
    pl.semaphore_wait(barrier, devices - 1)
    send_heads(0, 0)

    @pl.loop(1, pieces)
    def _(piece):
        attend(0, piece)
        send_heads(0, piece)

    for load in loads[2:-2]:
        load.wait()
    ids = jnp.concatenate([ids_ref[batch] for batch in range(batches)], axis=1)
    gates = jnp.concatenate([gates_ref[batch] for batch in range(batches)], axis=1)
    gates = gates.astype(jnp.float32)
    gates = gates / jnp.sum(gates, axis=0, keepdims=True)
    for expert in range(devices):
        share_out[expert] = jnp.sum(jnp.where(ids == expert, gates, 0.0), axis=0, keepdims=True)
    share_in[me] = share_out[me]

    @pl.loop(1, devices)
    def _(k):
        share_copy((me + k) % devices).start()

    attend(1, 0)
    send_heads(1, 0)
    take_heads(0)

    @pl.loop(1, pieces)
    def _(piece):
        attend(1, piece)
        send_heads(1, piece)

    @pl.loop(1, devices)
    def _(k):
        share_arrival((me + k) % devices).wait_recv()

    for load in loads[-2:]:
        load.wait()

    tile = 512

    def compute(blocks):
        for at, (batch, chip, which) in enumerate(blocks):
            xs[at * rows : (at + 1) * rows, :] = gathered[batch, chip, which]
            spread = jnp.broadcast_to(share_in[chip * 2 + which], (rows, share_in.shape[2]))
            lane = lax.broadcasted_iota(jnp.int32, spread.shape, 1)
            row = lax.broadcasted_iota(jnp.int32, spread.shape, 0)
            share = jnp.sum(
                jnp.where(lane == row + batch * rows, spread, 0.0), axis=-1, keepdims=True
            )
            sh[at * rows : (at + 1) * rows, :] = jnp.broadcast_to(share, spread.shape)
        taken = slice(0, len(blocks) * rows)
        gate = jnp.dot(xs[taken], gu[:, :hidden], preferred_element_type=jnp.float32)
        up = jnp.dot(xs[taken], gu[:, hidden:], preferred_element_type=jnp.float32)
        act[taken] = (gate / (1.0 + jnp.exp(-gate)) * up).astype(jnp.bfloat16)

        @pl.loop(0, width // tile)
        def _(j):
            cols = pl.ds(pl.multiple_of(j * tile, tile), tile)
            result = jnp.dot(act[taken], dn[:, cols], preferred_element_type=jnp.float32)
            for at, (batch, chip, which) in enumerate(blocks):
                share = sh[at * rows : (at + 1) * rows, :1]
                piece = result[at * rows : (at + 1) * rows]
                partial[batch, chip, which, :, cols] = (piece * share).astype(jnp.bfloat16)

    def gather_sum(batch, dest):
        return partial[batch, dest, core].astype(jnp.float32) + pairbuf[batch, dest].astype(
            jnp.float32
        )

    def around(dist):
        return chip_at(pos - dist), chip_at(pos + dist)

    def hand_on(dist, batch):
        origins = around(dist)
        for way in range(2):
            ag_copy(way, dist, batch, origins[way]).wait_recv()

            @pl.when((dist + 1 < far) | (batch == way))
            def _():
                ag_copy(way, dist + 1, batch, origins[way]).start()

            pair_copy(batch, origins[way]).start()

    def work(batch, origin):
        pair_arrival(batch, origin).wait_recv()
        compute([(batch, origin, which) for which in range(2)])
        sum_copy(batch, origin).start()

    def first(step):
        batch = step % 2
        return batch, chip_at(pos + (2 * batch - 1) * (step // 2 + 1))

    def second(step):
        batch = step % 2
        return batch, chip_at(pos - (2 * batch - 1) * (step // 2 + 1))

    def leaf(batch):
        way = 1 - batch
        dest = chip_at(pos + sign[way] * (far - 1))
        sum_copy(batch, dest).wait_recv()
        partial[batch, dest, core] = gather_sum(batch, dest).astype(jnp.bfloat16)
        rs_copy(way, 1, batch, dest).start()

    hand_on(1, 0)
    take_heads(1)

    @pl.loop(0, batches)
    def _(batch):
        work(batch, mine)

    work(*first(0))

    @pl.loop(1, 2 * (far - 1))
    def _(step):
        hand_on(step // 2 + 1, step % 2)
        work(*second(step - 1))
        work(*first(step))

    for batch in range(batches):
        leaf(batch)

    last = chip_at(pos + far)
    for batch in range(batches):
        ag_copy(batch, far, batch, last).wait_recv()
        pair_copy(batch, last).start()
    work(*second(2 * (far - 1) - 1))
    for batch in range(batches):
        pair_arrival(batch, last).wait_recv()
    compute([(batch, last, which) for batch in range(batches) for which in range(2)])
    for batch in range(batches):
        sum_copy(batch, last).start()

    for batch in range(batches):
        sum_copy(batch, last).wait_recv()
        partial[batch, last, core] = gather_sum(batch, last).astype(jnp.bfloat16)
        rs_copy(batch, 0, batch, last).start()

    def pass_on(way, turn, batch):
        dest = chip_at(pos + sign[way] * (far - turn))
        sum_copy(batch, dest).wait_recv()
        rs_copy(way, turn - 1, batch, dest).wait_recv()
        partial[batch, dest, core] = (
            gather_sum(batch, dest) + ringbuf[way, turn - 1, batch].astype(jnp.float32)
        ).astype(jnp.bfloat16)
        rs_copy(way, turn, batch, dest).start()

    @pl.loop(1, far - 1)
    def _(turn):
        for way in range(2):
            pass_on(way, turn + 1, 1 - way)
        for way in range(2):
            pass_on(way, turn, way)

    @pl.loop(1, devices)
    def _(k):
        share_copy((me + k) % devices).wait_send()
        for batch in range(batches):
            exchange(batch, (me + k) % devices).wait_send()

    for way in range(2):
        for batch in range(batches):
            ag_copy(way, 1, batch, mine).wait_send()
        ag_copy(way, far, way, mine).wait_send()

        @pl.loop(0, 2 * (far - 2))
        def _(step):
            ag_copy(way, step // 2 + 2, step % 2, mine).wait_send()

    @pl.loop(0, 2 * chips)
    def _(step):
        pair_copy(step % 2, step // 2).wait_send()
        sum_copy(step % 2, step // 2).wait_send()

    for way in range(2):
        pass_on(way, far - 1, way)

    for way in range(2):
        rs_copy(way, 0, way, mine).wait_send()

        @pl.loop(0, 2 * (far - 1) - 1)
        def _(step):
            turn = step // 2 + 1
            rs_copy(way, turn, (1 - way + step) % 2, mine).wait_send()

    for batch in range(batches):
        sum_copy(batch, mine).wait_recv()
        rs_copy(1 - batch, far - 1, batch, mine).wait_recv()
        stream[batch] = (
            stream[batch]
            + gather_sum(batch, mine)
            + ringbuf[1 - batch, far - 1, batch].astype(jnp.float32)
        )
    for batch in range(batches):
        rs_copy(batch, far - 1, batch, mine).wait_recv()
        out_ref[batch] = (
            stream[batch] + ringbuf[batch, far - 1, batch].astype(jnp.float32)
        ).astype(out_ref.dtype)
    for way in range(2):
        rs_copy(way, far - 1, way, mine).wait_send()


def fits(devices, rows, width, hidden):
    block = 2 * rows * (width + 128) * 2
    needed = 3 * devices * block + 3 * width * hidden * 2 + 8 * rows * width * 4
    return devices % 4 == 0 and 8 <= devices <= 64 and 2 * rows % 128 == 0 and needed < 48 * 1024 * 1024


def routed_layer(queries, keys_values, residual, norm_gain, ids, gates, gate_up, down_proj, kv_heads, devices):
    batches, rows, width = residual.shape
    length, part = queries.shape[1:]
    span = length // devices
    hidden = down_proj.shape[1]
    chips = devices // 2
    far = chips // 2
    dma = pltpu.SemaphoreType.DMA
    vmem = pl.BlockSpec(memory_space=pltpu.VMEM)
    anywhere = pl.BlockSpec(memory_space=pl.ANY)
    kind = jnp.bfloat16
    return pl.pallas_call(
        functools.partial(moe_kernel, chips),
        out_shape=pltpu.VMEM((batches, rows, width), kind),
        in_specs=[anywhere] * 8,
        out_specs=vmem,
        scratch_shapes=[
            pltpu.VMEM(queries.shape, kind),
            pltpu.VMEM(keys_values.shape, kind),
            pltpu.VMEM(residual.shape, kind),
            pltpu.VMEM((1, width), jnp.float32),
            pltpu.VMEM((batches, ids.shape[2], rows), jnp.int32),
            pltpu.VMEM((batches, ids.shape[2], rows), jnp.int32),
            pltpu.VMEM((batches, devices, span, part), kind),
            pltpu.VMEM((batches, devices // kv_heads, kv_heads, span, part), kind),
            pltpu.VMEM((batches, rows, width), jnp.float32),
            pltpu.VMEM((batches, chips, 2, rows, width), kind),
            pltpu.VMEM((batches, chips, 2, rows, width), kind),
            pltpu.VMEM((batches, chips, rows, width), kind),
            pltpu.VMEM((2, far, batches, rows, width), kind),
            pltpu.VMEM((width, 2 * hidden), kind),
            pltpu.VMEM((hidden, width), kind),
            pltpu.VMEM((4 * rows, width), kind),
            pltpu.VMEM((4 * rows, batches * rows), jnp.float32),
            pltpu.VMEM((4 * rows, hidden), kind),
            pltpu.VMEM((devices, 1, batches * rows), jnp.float32),
            pltpu.VMEM((devices, 1, batches * rows), jnp.float32),
            dma((2 * batches + 6,)),
            dma((devices,)), dma((devices,)),
            dma((batches, devices)), dma((batches, devices)),
            dma((2, far, batches)), dma((2, far, batches)),
            dma((batches, chips)), dma((batches, chips)),
            dma((batches, chips)), dma((batches, chips)),
            dma((2, far, batches)), dma((2, far, batches)),
        ],
        compiler_params=pltpu.CompilerParams(
            collective_id=0, has_side_effects=True, vmem_limit_bytes=56 * 1024 * 1024
        ),
    )(
        queries, keys_values, residual, norm_gain.reshape(1, width),
        jnp.transpose(ids, (0, 2, 1)), jnp.transpose(gates, (0, 2, 1)), gate_up, down_proj,
    )


def body(queries, keys_values, residual, norm_gain, gate_up, down_proj, expert_ids, expert_gates):
    devices = lax.axis_size("dev")
    me = lax.axis_index("dev")
    model_width = residual.shape[2]
    kv_heads = model_width // queries.shape[3]
    experts = devices * gate_up.shape[0]
    batches, unit, length, feat_width = queries.shape
    positions = length // devices
    if batches == 2 and fits(devices, residual.shape[1], model_width, down_proj.shape[1]):
        return routed_layer(
            queries[:, 0], keys_values[:, 0], residual, norm_gain, expert_ids, expert_gates,
            gate_up, down_proj, kv_heads, devices,
        )
    weights = dense_shares(expert_ids, expert_gates, experts)
    blended = attend_local(queries, keys_values)
    weights = lax.all_gather(weights, "dev", axis=1, tiled=True)
    mine = jnp.sum(
        jnp.where(jnp.arange(experts, dtype=jnp.int32) == me, weights, 0.0), axis=-1, keepdims=True
    )
    pieces = []
    for batch_index in range(batches):
        outgoing_rows = blended[batch_index].reshape(1, devices, positions, feat_width)
        arrived_rows = lax.all_to_all(outgoing_rows, "dev", split_axis=1, concat_axis=1, tiled=True)
        attn_rows = to_owners(arrived_rows, kv_heads)
        stream, normed = prepare(attn_rows[0], residual[batch_index], norm_gain)
        rows_in = lax.all_gather(normed, "dev", axis=0, tiled=True)
        partial = run_expert(rows_in, gate_up, down_proj, mine[batch_index])
        summed = lax.psum_scatter(partial, "dev", scatter_dimension=0, tiled=True)
        pieces.append((stream + summed.astype(jnp.float32)).astype(jnp.bfloat16))
    return jnp.stack(pieces, axis=0)


def solution(mesh):
    in_specs = (
        P(None, ("groups", "dev"), None, None),
        P(None, ("groups", "dev"), None, None, None),
        P(None, ("groups", "dev"), None),
        P(),
        P("dev", None, None),
        P("dev", None, None),
        P(None, ("groups", "dev"), None),
        P(None, ("groups", "dev"), None),
    )
    out_specs = P(None, ("groups", "dev"), None)
    return jax.shard_map(body, mesh=mesh, in_specs=in_specs, out_specs=out_specs, check_vma=False)
```

```python
import functools
import math

import jax
import jax.numpy as jnp
from jax import lax
from jax.experimental import pallas as pl
from jax.experimental.pallas import tpu as pltpu
from jax.sharding import PartitionSpec as P


def attend_pair(heads, pair_rows, keys, values):
    length = pair_rows.shape[0]
    context, head_size = keys.shape
    past = context - length
    query = jnp.concatenate(
        [pair_rows[:, head * head_size : (head + 1) * head_size] for head in range(heads)], axis=0
    )
    scores = lax.dot_general(
        query, keys, (((1,), (1,)), ((), ())), preferred_element_type=jnp.float32
    )
    rate = math.log2(math.e) / math.sqrt(head_size)
    old, new = scores[:, :past], scores[:, past:]
    row = lax.broadcasted_iota(jnp.int32, new.shape, 0) % length
    col = lax.broadcasted_iota(jnp.int32, new.shape, 1)
    new = jnp.where(col <= row, new, -1e30)
    highest = jnp.maximum(
        jnp.max(old, axis=-1, keepdims=True), jnp.max(new, axis=-1, keepdims=True)
    )
    old = jnp.exp2((old - highest) * rate)
    new = jnp.exp2((new - highest) * rate)
    totals = jnp.sum(old, axis=-1, keepdims=True) + jnp.sum(new, axis=-1, keepdims=True)
    blended = jnp.dot(
        old.astype(jnp.bfloat16), values[:past], preferred_element_type=jnp.float32
    ) + jnp.dot(new.astype(jnp.bfloat16), values[past:], preferred_element_type=jnp.float32)
    return blended * (1.0 / totals)


def attend_kernel(heads, q_ref, kv_ref, out_ref):
    length = q_ref.shape[1]
    head_size = kv_ref.shape[4]
    blended = attend_pair(heads, q_ref[0], kv_ref[0, 0, 0], kv_ref[0, 0, 1])
    for head in range(heads):
        out_ref[0, :, head * head_size : (head + 1) * head_size] = blended[
            head * length : (head + 1) * length
        ].astype(jnp.bfloat16)


def attend_local(queries, keys_values):
    batches, unit, length, feat_width = queries.shape
    context, head_size = keys_values.shape[3:]
    heads = 2
    wide = heads * head_size
    return pl.pallas_call(
        functools.partial(attend_kernel, heads),
        grid=(batches, feat_width // wide),
        out_shape=jax.ShapeDtypeStruct((batches, length, feat_width), jnp.bfloat16),
        in_specs=[
            pl.BlockSpec((1, length, wide), lambda b, h: (b, 0, h)),
            pl.BlockSpec((1, 1, 2, context, head_size), lambda b, h: (b, 0, 0, 0, 0)),
        ],
        out_specs=pl.BlockSpec((1, length, wide), lambda b, h: (b, 0, h)),
        compiler_params=pltpu.CompilerParams(vmem_limit_bytes=40 * 1024 * 1024),
    )(queries.reshape(batches, length, feat_width), keys_values)


def to_owners(exchanged, kv_heads):
    batches, sources, positions, feat_width = exchanged.shape
    grouped = exchanged.reshape(batches, sources // kv_heads, kv_heads, positions, feat_width)
    grouped = jnp.transpose(grouped, (0, 1, 3, 2, 4))
    return grouped.reshape(batches, sources // kv_heads * positions, kv_heads * feat_width)


def prepare(attn_rows, residual, norm_gain):
    stream = residual.astype(jnp.float32) + attn_rows.astype(jnp.float32)
    meansq = jnp.mean(stream * stream, axis=-1, keepdims=True)
    normed = (stream * lax.rsqrt(meansq + 1e-06) * norm_gain).astype(jnp.bfloat16)
    return stream, normed


def dense_shares(expert_ids, expert_gates, experts):
    shares = expert_gates.astype(jnp.float32)
    shares = shares / jnp.sum(shares, axis=-1, keepdims=True)
    named = expert_ids[..., None] == jnp.arange(experts, dtype=jnp.int32)
    return jnp.sum(jnp.where(named, shares[..., None], 0.0), axis=-2)


def run_expert(rows_in, gate_up, down_proj, weight):
    hidden_width = down_proj.shape[1]
    projected = jnp.dot(rows_in, gate_up[0], preferred_element_type=jnp.float32)
    hidden = (jax.nn.silu(projected[:, :hidden_width]) * projected[:, hidden_width:]).astype(
        jnp.bfloat16
    )
    output = jnp.dot(hidden, down_proj[0], preferred_element_type=jnp.float32)
    return (output * weight).astype(jnp.bfloat16)


MESH = pl.DeviceIdType.MESH


def moe_kernel(
    chips, q_hbm, kv_hbm, res_hbm, gain_hbm, ids_hbm, gates_hbm, gu_hbm, dn_hbm, out_ref,
    q_ref, kv_ref, res_ref, gain_ref, ids_ref, gates_ref,
    heads_ref, attn, stream, gathered, partial, pairbuf, ringbuf, gu, dn, xs, sh, act, share_out, share_in,
    load_sem, sh_send, sh_recv, ex_send, ex_recv, ag_send, ag_recv, agp_send, agp_recv, rsp_send, rsp_recv, rs_send, rs_recv,
    half_recv,
):
    batches, rows, width = res_ref.shape
    devices = 2 * chips
    part = attn.shape[3]
    kv_heads = width // part
    hidden = dn.shape[0]
    far = chips // 2
    me = lax.axis_index("dev")
    core = me % 2
    mine = me // 2
    odd = mine % 2
    pos = odd * ((mine + 1) // 2) + (1 - odd) * ((chips - mine // 2) % chips)

    def chip_at(place):
        q = (place + 2 * chips) % chips
        upper = q // (far + 1)
        some = (q + chips - 1) // chips
        return some * ((1 - upper) * (2 * q - 1) + upper * 2 * (chips - q))

    partner = mine * 2 + (1 - core)
    ahead = (chip_at(pos + 1) * 2 + core, chip_at(pos - 1) * 2 + core)
    sign = (1, -1)
    halves = (slice(0, rows // 2), slice(rows // 2, rows))

    def remote(src, dst, send, recv, target):
        return pltpu.make_async_remote_copy(
            src_ref=src, dst_ref=dst, send_sem=send, recv_sem=recv,
            device_id={"dev": target}, device_id_type=MESH,
        )

    def ag_copy(way, dist, batch, origin, half):
        slot = gathered.at[batch, origin, core, halves[half]]
        return remote(slot, slot, ag_send, ag_recv.at[way, dist - 1, batch, half], ahead[way])

    def pair_copy(batch, origin, half):
        slot = gathered.at[batch, origin, core, halves[half]]
        return remote(slot, slot, agp_send, agp_recv.at[batch, origin], partner)

    def pair_arrival(batch, origin):
        slot = gathered.at[batch, origin, 1 - core]
        return remote(slot, slot, agp_send, agp_recv.at[batch, origin], partner)

    def sum_copy(batch, dest):
        return remote(
            partial.at[batch, dest, 1 - core], pairbuf.at[batch, dest],
            rsp_send, rsp_recv.at[batch, dest], partner,
        )

    def rs_copy(way, turn, batch, dest):
        return remote(
            partial.at[batch, dest, core], ringbuf.at[way, turn, batch],
            rs_send, rs_recv.at[way, turn, batch], ahead[way],
        )

    def half_copy(way, late, half, dest):
        turn, some = far - 2 + late, halves[half]
        return remote(
            partial.at[way, dest, core, some], ringbuf.at[way, turn, way, some],
            rs_send, half_recv.at[way, late, half], ahead[way],
        )

    def exchange(batch, target, cols):
        return remote(
            heads_ref.at[batch, target, :, cols], attn.at[batch, me, :, cols],
            ex_send.at[batch], ex_recv.at[batch], target,
        )

    def exchanged(batch):
        slots = attn.at[batch, pl.ds(0, devices - 1)]
        return remote(slots, slots, ex_send.at[batch], ex_recv.at[batch], partner)

    def share_copy(target):
        return remote(share_out.at[target], share_in.at[me], sh_send, sh_recv, target)

    def shared():
        slots = share_in.at[pl.ds(0, devices - 1)]
        return remote(slots, slots, sh_send, sh_recv, partner)

    barrier = pltpu.get_barrier_semaphore()

    @pl.loop(1, devices)
    def _(k):
        target = (me + k) % devices
        pl.semaphore_signal(barrier, inc=1, device_id={"dev": target}, device_id_type=MESH)

    pairs = [(q_hbm.at[0], q_ref.at[0]), (kv_hbm.at[0], kv_ref.at[0])]
    pairs += [(ids_hbm, ids_ref), (gates_hbm, gates_ref), (gain_hbm, gain_ref), (res_hbm, res_ref)]
    for batch in range(1, batches):
        pairs += [(q_hbm.at[batch], q_ref.at[batch]), (kv_hbm.at[batch], kv_ref.at[batch])]
    pairs += [(gu_hbm.at[0], gu), (dn_hbm.at[0], dn)]
    loads = [
        pltpu.make_async_copy(src, dst, load_sem.at[at]) for at, (src, dst) in enumerate(pairs)
    ]
    for load in loads:
        load.start()

    head_size = kv_ref.shape[3]
    length = q_ref.shape[1]

    wide = 2 * head_size
    pieces = part // wide

    def columns(piece):
        return pl.ds(pl.multiple_of(piece * wide, wide), wide)

    def attend(batch, piece):
        cols = columns(piece)
        blended = attend_pair(2, q_ref[batch, :, cols], kv_ref[batch, 0], kv_ref[batch, 1])
        for head in range(2):
            at = pl.ds(pl.multiple_of(piece * wide + head * head_size, head_size), head_size)
            heads_ref[batch, :, :, at] = blended[head * length : (head + 1) * length].reshape(
                devices, length // devices, head_size
            ).astype(jnp.bfloat16)

    def send_heads(batch, portion):
        cols = slice(portion * part // 2, (portion + 1) * part // 2)

        @pl.loop(1, devices)
        def _(k):
            exchange(batch, (me + k) % devices, cols).start()

    def take_heads(batch):
        attn[batch, me] = heads_ref[batch, me]
        exchanged(batch).wait_recv()
        arrived = attn[batch].reshape(devices // kv_heads, kv_heads, rows * kv_heads // devices, part)
        squares = jnp.zeros((rows, 1), jnp.float32)
        for head in range(kv_heads):
            cols = slice(head * part, (head + 1) * part)
            added = arrived[:, head].astype(jnp.float32).reshape(rows, part)
            added = added + res_ref[batch, :, cols].astype(jnp.float32)
            stream[batch, :, cols] = added
            squares = squares + jnp.sum(added * added, axis=-1, keepdims=True)
        scale = lax.rsqrt(squares / width + 1e-06)
        gathered[batch, mine, core] = (stream[batch] * scale * gain_ref[...]).astype(jnp.bfloat16)
        for half in range(2):
            for way in range(2):
                ag_copy(way, 1, batch, mine, half).start()
            pair_copy(batch, mine, half).start()

    for load in loads[:2]:
        load.wait()

    @pl.loop(0, pieces)
    def _(piece):
        attend(0, piece)

        @pl.when(piece == pieces // 2 - 1)
        def _():
            pl.semaphore_wait(barrier, devices - 1)
            send_heads(0, 0)

    send_heads(0, 1)

    for load in loads[2:-2]:
        load.wait()
    ids = jnp.concatenate([ids_ref[batch] for batch in range(batches)], axis=1)
    gates = jnp.concatenate([gates_ref[batch] for batch in range(batches)], axis=1)
    gates = gates.astype(jnp.float32)
    gates = gates / jnp.sum(gates, axis=0, keepdims=True)
    for expert in range(devices):
        share_out[expert] = jnp.sum(jnp.where(ids == expert, gates, 0.0), axis=0, keepdims=True)
    share_in[me] = share_out[me]

    @pl.loop(1, devices)
    def _(k):
        share_copy((me + k) % devices).start()

    @pl.loop(0, pieces)
    def _(piece):
        attend(1, piece)

        @pl.when(piece == pieces // 2 - 1)
        def _():
            take_heads(0)
            send_heads(1, 0)

    send_heads(1, 1)

    shared().wait_recv()
    for load in loads[-2:]:
        load.wait()

    tile = 512

    def compute(blocks):
        for at, (batch, chip, which) in enumerate(blocks):
            xs[at * rows : (at + 1) * rows, :] = gathered[batch, chip, which]
            spread = jnp.broadcast_to(share_in[chip * 2 + which], (rows, share_in.shape[2]))
            lane = lax.broadcasted_iota(jnp.int32, spread.shape, 1)
            row = lax.broadcasted_iota(jnp.int32, spread.shape, 0)
            share = jnp.sum(
                jnp.where(lane == row + batch * rows, spread, 0.0), axis=-1, keepdims=True
            )
            sh[at * rows : (at + 1) * rows, :] = jnp.broadcast_to(share, spread.shape)
        taken = slice(0, len(blocks) * rows)
        gate = jnp.dot(xs[taken], gu[:, :hidden], preferred_element_type=jnp.float32)
        up = jnp.dot(xs[taken], gu[:, hidden:], preferred_element_type=jnp.float32)
        act[taken] = (gate / (1.0 + jnp.exp(-gate)) * up).astype(jnp.bfloat16)

        @pl.loop(0, width // tile)
        def _(j):
            cols = pl.ds(pl.multiple_of(j * tile, tile), tile)
            result = jnp.dot(act[taken], dn[:, cols], preferred_element_type=jnp.float32)
            for at, (batch, chip, which) in enumerate(blocks):
                share = sh[at * rows : (at + 1) * rows, :1]
                piece = result[at * rows : (at + 1) * rows]
                partial[batch, chip, which, :, cols] = (piece * share).astype(jnp.bfloat16)

    def gather_sum(batch, dest):
        return partial[batch, dest, core].astype(jnp.float32) + pairbuf[batch, dest].astype(
            jnp.float32
        )

    def around(dist):
        return chip_at(pos - dist), chip_at(pos + dist)

    def arrive(way, dist, batch, half):
        origin = around(dist)[way]
        ag_copy(way, dist, batch, origin, half).wait_recv()
        if isinstance(dist, int):
            if dist + 1 < far or (dist < far and batch == way):
                ag_copy(way, dist + 1, batch, origin, half).start()
        else:

            @pl.when((dist + 1 < far) | (batch == way))
            def _():
                ag_copy(way, dist + 1, batch, origin, half).start()

        pair_copy(batch, origin, half).start()

    def hand_on(dist, batch):
        for half in range(2):
            for way in range(2):
                arrive(way, dist, batch, half)

    def work(batch, origin):
        pair_arrival(batch, origin).wait_recv()
        compute([(batch, origin, which) for which in range(2)])
        sum_copy(batch, origin).start()

    def place(step):
        batch = (step + 1) % 2
        return batch, (step + 1) // 2 + 1 - batch

    def first(step):
        batch, dist = place(step)
        return batch, chip_at(pos - dist)

    def second(step):
        batch, dist = place(step)
        return batch, chip_at(pos + dist)

    def leaf(batch):
        way = 1 - batch
        dest = chip_at(pos + sign[way] * (far - 1))
        sum_copy(batch, dest).wait_recv()
        partial[batch, dest, core] = gather_sum(batch, dest).astype(jnp.bfloat16)
        rs_copy(way, 1, batch, dest).start()

    last = chip_at(pos + far)

    def turn_round(batch):
        sum_copy(batch, last).wait_recv()
        partial[batch, last, core] = gather_sum(batch, last).astype(jnp.bfloat16)
        rs_copy(batch, 0, batch, last).start()

    hand_on(1, 0)
    work(0, mine)
    take_heads(1)
    for origin in around(1):
        work(0, origin)

    @pl.loop(1, 2 * (far - 2) + 1)
    def _(step):
        batch, dist = place(step)
        hand_on(dist, batch)
        work(*second(step - 1))
        work(*first(step))

    for half in range(2):
        arrive(0, far, 0, half)
        arrive(1, far - 1, 1, half)
    work(*second(2 * (far - 2)))
    work(0, last)
    leaf(0)
    work(1, around(far - 1)[1])
    turn_round(0)
    for half in range(2):
        arrive(0, far - 1, 1, half)
        arrive(1, far, 1, half)
    leaf(1)
    work(1, around(far - 1)[0])
    work(1, last)
    turn_round(1)

    def pass_on(way, turn, batch):
        dest = chip_at(pos + sign[way] * (far - turn))
        sum_copy(batch, dest).wait_recv()
        rs_copy(way, turn - 1, batch, dest).wait_recv()
        partial[batch, dest, core] = (
            gather_sum(batch, dest) + ringbuf[way, turn - 1, batch].astype(jnp.float32)
        ).astype(jnp.bfloat16)
        rs_copy(way, turn, batch, dest).start()

    @pl.loop(1, far - 2)
    def _(turn):
        pass_on(1, turn + 1, 0)
        pass_on(0, turn, 0)
        pass_on(0, turn + 1, 1)
        pass_on(1, turn, 1)

    def pass_half(way, late, half):
        dest = chip_at(pos + sign[way] * (2 - late))
        some = halves[half]
        if late:
            half_copy(way, 0, half, dest).wait_recv()
        partial[way, dest, core, some] = (
            partial[way, dest, core, some].astype(jnp.float32)
            + pairbuf[way, dest, some].astype(jnp.float32)
            + ringbuf[way, far - 3 + late, way, some].astype(jnp.float32)
        ).astype(jnp.bfloat16)
        half_copy(way, late, half, dest).start()

    def pass_late(way):
        dest = chip_at(pos + sign[way] * 2)
        sum_copy(way, dest).wait_recv()
        rs_copy(way, far - 3, way, dest).wait_recv()
        for half in range(2):
            pass_half(way, 0, half)

    pass_on(1, far - 1, 0)
    pass_late(0)
    pass_on(0, far - 1, 1)
    pass_late(1)
    for way in range(2):
        sum_copy(way, chip_at(pos + sign[way])).wait_recv()

    for half in range(2):
        for way in range(2):
            pass_half(way, 1, half)

    shared().wait_send()
    for batch in range(batches):
        exchanged(batch).wait_send()
    some = gathered.at[0, pl.ds(0, chips - 1)]
    remote(some, some, ag_send, sh_recv, partner).wait_send()
    remote(gathered.at[0], gathered.at[0], agp_send, sh_recv, partner).wait_send()
    remote(partial.at[0], partial.at[0], rsp_send, sh_recv, partner).wait_send()

    for batch in range(batches):
        sum_copy(batch, mine).wait_recv()
        rs_copy(1 - batch, far - 1, batch, mine).wait_recv()
        stream[batch] = (
            stream[batch]
            + gather_sum(batch, mine)
            + ringbuf[1 - batch, far - 1, batch].astype(jnp.float32)
        )
    for half in range(2):
        some = halves[half]
        for batch in range(batches):
            half_copy(batch, 1, half, mine).wait_recv()
            out_ref[batch, some] = (
                stream[batch, some] + ringbuf[batch, far - 1, batch, some].astype(jnp.float32)
            ).astype(out_ref.dtype)
    some = partial.at[0, pl.ds(0, chips - 1)]
    remote(some, some, rs_send, sh_recv, partner).wait_send()


def fits(devices, rows, width, hidden):
    block = 2 * rows * (width + 128) * 2
    needed = 3 * devices * block + 3 * width * hidden * 2 + 8 * rows * width * 4
    return devices % 4 == 0 and 12 <= devices <= 64 and rows % 32 == 0 and 2 * rows % 128 == 0 and needed < 48 * 1024 * 1024


def routed_layer(queries, keys_values, residual, norm_gain, ids, gates, gate_up, down_proj, kv_heads, devices):
    batches, rows, width = residual.shape
    length, part = queries.shape[1:]
    span = length // devices
    hidden = down_proj.shape[1]
    chips = devices // 2
    far = chips // 2
    dma = pltpu.SemaphoreType.DMA
    vmem = pl.BlockSpec(memory_space=pltpu.VMEM)
    anywhere = pl.BlockSpec(memory_space=pl.ANY)
    kind = jnp.bfloat16
    return pl.pallas_call(
        functools.partial(moe_kernel, chips),
        out_shape=pltpu.VMEM((batches, rows, width), kind),
        in_specs=[anywhere] * 8,
        out_specs=vmem,
        scratch_shapes=[
            pltpu.VMEM(queries.shape, kind),
            pltpu.VMEM(keys_values.shape, kind),
            pltpu.VMEM(residual.shape, kind),
            pltpu.VMEM((1, width), jnp.float32),
            pltpu.VMEM((batches, ids.shape[2], rows), jnp.int32),
            pltpu.VMEM((batches, ids.shape[2], rows), jnp.int32),
            pltpu.VMEM((batches, devices, span, part), kind),
            pltpu.VMEM((batches, devices, span, part), kind),
            pltpu.VMEM((batches, rows, width), jnp.float32),
            pltpu.VMEM((batches, chips, 2, rows, width), kind),
            pltpu.VMEM((batches, chips, 2, rows, width), kind),
            pltpu.VMEM((batches, chips, rows, width), kind),
            pltpu.VMEM((2, far, batches, rows, width), kind),
            pltpu.VMEM((width, 2 * hidden), kind),
            pltpu.VMEM((hidden, width), kind),
            pltpu.VMEM((4 * rows, width), kind),
            pltpu.VMEM((4 * rows, batches * rows), jnp.float32),
            pltpu.VMEM((4 * rows, hidden), kind),
            pltpu.VMEM((devices, 1, batches * rows), jnp.float32),
            pltpu.VMEM((devices, 1, batches * rows), jnp.float32),
            dma((2 * batches + 6,)),
            dma, dma,
            dma((batches,)), dma((batches,)),
            dma, dma((2, far, batches, 2)),
            dma, dma((batches, chips)),
            dma, dma((batches, chips)),
            dma, dma((2, far, batches)),
            dma((2, 2, 2)),
        ],
        compiler_params=pltpu.CompilerParams(
            collective_id=0, has_side_effects=True, vmem_limit_bytes=56 * 1024 * 1024
        ),
    )(
        queries, keys_values, residual, norm_gain.reshape(1, width),
        jnp.transpose(ids, (0, 2, 1)), jnp.transpose(gates, (0, 2, 1)), gate_up, down_proj,
    )


def body(queries, keys_values, residual, norm_gain, gate_up, down_proj, expert_ids, expert_gates):
    devices = lax.axis_size("dev")
    me = lax.axis_index("dev")
    model_width = residual.shape[2]
    kv_heads = model_width // queries.shape[3]
    experts = devices * gate_up.shape[0]
    batches, unit, length, feat_width = queries.shape
    positions = length // devices
    if batches == 2 and fits(devices, residual.shape[1], model_width, down_proj.shape[1]):
        return routed_layer(
            queries[:, 0], keys_values[:, 0], residual, norm_gain, expert_ids, expert_gates,
            gate_up, down_proj, kv_heads, devices,
        )
    weights = dense_shares(expert_ids, expert_gates, experts)
    blended = attend_local(queries, keys_values)
    weights = lax.all_gather(weights, "dev", axis=1, tiled=True)
    mine = jnp.sum(
        jnp.where(jnp.arange(experts, dtype=jnp.int32) == me, weights, 0.0), axis=-1, keepdims=True
    )
    pieces = []
    for batch_index in range(batches):
        outgoing_rows = blended[batch_index].reshape(1, devices, positions, feat_width)
        arrived_rows = lax.all_to_all(outgoing_rows, "dev", split_axis=1, concat_axis=1, tiled=True)
        attn_rows = to_owners(arrived_rows, kv_heads)
        stream, normed = prepare(attn_rows[0], residual[batch_index], norm_gain)
        rows_in = lax.all_gather(normed, "dev", axis=0, tiled=True)
        partial = run_expert(rows_in, gate_up, down_proj, mine[batch_index])
        summed = lax.psum_scatter(partial, "dev", scatter_dimension=0, tiled=True)
        pieces.append((stream + summed.astype(jnp.float32)).astype(jnp.bfloat16))
    return jnp.stack(pieces, axis=0)


def solution(mesh):
    in_specs = (
        P(None, ("groups", "dev"), None, None),
        P(None, ("groups", "dev"), None, None, None),
        P(None, ("groups", "dev"), None),
        P(),
        P("dev", None, None),
        P("dev", None, None),
        P(None, ("groups", "dev"), None),
        P(None, ("groups", "dev"), None),
    )
    out_specs = P(None, ("groups", "dev"), None)
    return jax.shard_map(body, mesh=mesh, in_specs=in_specs, out_specs=out_specs, check_vma=False)
```

```python
import functools
import math

import jax
import jax.numpy as jnp
from jax import lax
from jax.experimental import pallas as pl
from jax.experimental.pallas import tpu as pltpu
from jax.sharding import PartitionSpec as P


def attend_pair(heads, pair_rows, keys, values):
    length = pair_rows.shape[0]
    context, head_size = keys.shape
    past = context - length
    query = jnp.concatenate(
        [pair_rows[:, head * head_size : (head + 1) * head_size] for head in range(heads)], axis=0
    )
    scores = lax.dot_general(
        query, keys, (((1,), (1,)), ((), ())), preferred_element_type=jnp.float32
    )
    rate = math.log2(math.e) / math.sqrt(head_size)
    old, new = scores[:, :past], scores[:, past:]
    row = lax.broadcasted_iota(jnp.int32, new.shape, 0) % length
    col = lax.broadcasted_iota(jnp.int32, new.shape, 1)
    new = jnp.where(col <= row, new, -1e30)
    highest = jnp.maximum(
        jnp.max(old, axis=-1, keepdims=True), jnp.max(new, axis=-1, keepdims=True)
    )
    old = jnp.exp2((old - highest) * rate)
    new = jnp.exp2((new - highest) * rate)
    totals = jnp.sum(old, axis=-1, keepdims=True) + jnp.sum(new, axis=-1, keepdims=True)
    blended = jnp.dot(
        old.astype(jnp.bfloat16), values[:past], preferred_element_type=jnp.float32
    ) + jnp.dot(new.astype(jnp.bfloat16), values[past:], preferred_element_type=jnp.float32)
    return blended * (1.0 / totals)


def attend_kernel(heads, q_ref, kv_ref, out_ref):
    length = q_ref.shape[1]
    head_size = kv_ref.shape[4]
    blended = attend_pair(heads, q_ref[0], kv_ref[0, 0, 0], kv_ref[0, 0, 1])
    for head in range(heads):
        out_ref[0, :, head * head_size : (head + 1) * head_size] = blended[
            head * length : (head + 1) * length
        ].astype(jnp.bfloat16)


def attend_local(queries, keys_values):
    batches, unit, length, feat_width = queries.shape
    context, head_size = keys_values.shape[3:]
    heads = 2
    wide = heads * head_size
    return pl.pallas_call(
        functools.partial(attend_kernel, heads),
        grid=(batches, feat_width // wide),
        out_shape=jax.ShapeDtypeStruct((batches, length, feat_width), jnp.bfloat16),
        in_specs=[
            pl.BlockSpec((1, length, wide), lambda b, h: (b, 0, h)),
            pl.BlockSpec((1, 1, 2, context, head_size), lambda b, h: (b, 0, 0, 0, 0)),
        ],
        out_specs=pl.BlockSpec((1, length, wide), lambda b, h: (b, 0, h)),
        compiler_params=pltpu.CompilerParams(vmem_limit_bytes=40 * 1024 * 1024),
    )(queries.reshape(batches, length, feat_width), keys_values)


def to_owners(exchanged, kv_heads):
    batches, sources, positions, feat_width = exchanged.shape
    grouped = exchanged.reshape(batches, sources // kv_heads, kv_heads, positions, feat_width)
    grouped = jnp.transpose(grouped, (0, 1, 3, 2, 4))
    return grouped.reshape(batches, sources // kv_heads * positions, kv_heads * feat_width)


def prepare(attn_rows, residual, norm_gain):
    stream = residual.astype(jnp.float32) + attn_rows.astype(jnp.float32)
    meansq = jnp.mean(stream * stream, axis=-1, keepdims=True)
    normed = (stream * lax.rsqrt(meansq + 1e-06) * norm_gain).astype(jnp.bfloat16)
    return stream, normed


def dense_shares(expert_ids, expert_gates, experts):
    shares = expert_gates.astype(jnp.float32)
    shares = shares / jnp.sum(shares, axis=-1, keepdims=True)
    named = expert_ids[..., None] == jnp.arange(experts, dtype=jnp.int32)
    return jnp.sum(jnp.where(named, shares[..., None], 0.0), axis=-2)


def run_expert(rows_in, gate_up, down_proj, weight):
    hidden_width = down_proj.shape[1]
    projected = jnp.dot(rows_in, gate_up[0], preferred_element_type=jnp.float32)
    hidden = (jax.nn.silu(projected[:, :hidden_width]) * projected[:, hidden_width:]).astype(
        jnp.bfloat16
    )
    output = jnp.dot(hidden, down_proj[0], preferred_element_type=jnp.float32)
    return (output * weight).astype(jnp.bfloat16)


MESH = pl.DeviceIdType.MESH


def moe_kernel(
    chips, q_hbm, kv_hbm, res_hbm, gain_hbm, ids_hbm, gates_hbm, gu_hbm, dn_hbm, out_ref,
    q_ref, kv_ref, res_ref, gain_ref, ids_ref, gates_ref,
    heads_ref, attn, stream, gathered, partial, pairbuf, ringbuf, gu, dn, xs, sh, act, share_out, share_in,
    load_sem, sh_send, sh_recv, ex_send, ex_recv, ag_send, ag_recv, agp_send, agp_recv, rsp_send, rsp_recv, rs_send, rs_recv,
    half_recv,
):
    batches, rows, width = res_ref.shape
    devices = 2 * chips
    part = attn.shape[3]
    kv_heads = width // part
    hidden = dn.shape[0]
    far = chips // 2
    me = lax.axis_index("dev")
    core = me % 2
    mine = me // 2
    odd = mine % 2
    pos = odd * ((mine + 1) // 2) + (1 - odd) * ((chips - mine // 2) % chips)

    def chip_at(place):
        q = (place + 2 * chips) % chips
        upper = q // (far + 1)
        some = (q + chips - 1) // chips
        return some * ((1 - upper) * (2 * q - 1) + upper * 2 * (chips - q))

    partner = mine * 2 + (1 - core)
    ahead = (chip_at(pos + 1) * 2 + core, chip_at(pos - 1) * 2 + core)
    sign = (1, -1)
    halves = (slice(0, rows // 2), slice(rows // 2, rows))

    def remote(src, dst, send, recv, target):
        return pltpu.make_async_remote_copy(
            src_ref=src, dst_ref=dst, send_sem=send, recv_sem=recv,
            device_id={"dev": target}, device_id_type=MESH,
        )

    def ag_copy(way, dist, batch, origin, half):
        slot = gathered.at[batch, origin, core, halves[half]]
        return remote(slot, slot, ag_send, ag_recv.at[way, dist - 1, batch, half], ahead[way])

    def pair_copy(batch, origin, half):
        slot = gathered.at[batch, origin, core, halves[half]]
        return remote(slot, slot, agp_send, agp_recv.at[batch, origin], partner)

    def pair_arrival(batch, origin):
        slot = gathered.at[batch, origin, 1 - core]
        return remote(slot, slot, agp_send, agp_recv.at[batch, origin], partner)

    def sum_copy(batch, dest):
        return remote(
            partial.at[batch, dest, 1 - core], pairbuf.at[batch, dest],
            rsp_send, rsp_recv.at[batch, dest], partner,
        )

    def rs_copy(way, turn, batch, dest):
        return remote(
            partial.at[batch, dest, core], ringbuf.at[way, turn, batch],
            rs_send, rs_recv.at[way, turn, batch], ahead[way],
        )

    def half_copy(way, late, half, dest):
        turn, some = far - 2 + late, halves[half]
        return remote(
            partial.at[way, dest, core, some], ringbuf.at[way, turn, way, some],
            rs_send, half_recv.at[way, late, half], ahead[way],
        )

    def exchange(batch, target, cols):
        return remote(
            heads_ref.at[batch, target, :, cols], attn.at[batch, me, :, cols],
            ex_send.at[batch], ex_recv.at[batch], target,
        )

    def exchanged(batch):
        slots = attn.at[batch, pl.ds(0, devices - 1)]
        return remote(slots, slots, ex_send.at[batch], ex_recv.at[batch], partner)

    def share_copy(target):
        return remote(share_out.at[target], share_in.at[me], sh_send, sh_recv, target)

    def shared():
        slots = share_in.at[pl.ds(0, devices - 1)]
        return remote(slots, slots, sh_send, sh_recv, partner)

    barrier = pltpu.get_barrier_semaphore()

    @pl.loop(1, devices)
    def _(k):
        target = (me + k) % devices
        pl.semaphore_signal(barrier, inc=1, device_id={"dev": target}, device_id_type=MESH)

    pairs = [(q_hbm.at[0], q_ref.at[0]), (kv_hbm.at[0], kv_ref.at[0])]
    pairs += [(ids_hbm, ids_ref), (gates_hbm, gates_ref), (gain_hbm, gain_ref), (res_hbm, res_ref)]
    for batch in range(1, batches):
        pairs += [(q_hbm.at[batch], q_ref.at[batch]), (kv_hbm.at[batch], kv_ref.at[batch])]
    pairs += [(gu_hbm.at[0], gu), (dn_hbm.at[0], dn)]
    loads = [
        pltpu.make_async_copy(src, dst, load_sem.at[at]) for at, (src, dst) in enumerate(pairs)
    ]
    for load in loads:
        load.start()

    head_size = kv_ref.shape[3]
    length = q_ref.shape[1]

    wide = 2 * head_size
    pieces = part // wide

    def columns(piece):
        return pl.ds(pl.multiple_of(piece * wide, wide), wide)

    def attend(batch, piece):
        cols = columns(piece)
        blended = attend_pair(2, q_ref[batch, :, cols], kv_ref[batch, 0], kv_ref[batch, 1])
        for head in range(2):
            at = pl.ds(pl.multiple_of(piece * wide + head * head_size, head_size), head_size)
            heads_ref[batch, :, :, at] = blended[head * length : (head + 1) * length].reshape(
                devices, length // devices, head_size
            ).astype(jnp.bfloat16)

    def send_heads(batch, portion):
        cols = slice(portion * part // 2, (portion + 1) * part // 2)

        @pl.loop(1, devices)
        def _(k):
            exchange(batch, (me + k) % devices, cols).start()

    def take_heads(batch):
        attn[batch, me] = heads_ref[batch, me]
        exchanged(batch).wait_recv()
        arrived = attn[batch].reshape(devices // kv_heads, kv_heads, rows * kv_heads // devices, part)
        squares = jnp.zeros((rows, 1), jnp.float32)
        for head in range(kv_heads):
            cols = slice(head * part, (head + 1) * part)
            added = arrived[:, head].astype(jnp.float32).reshape(rows, part)
            added = added + res_ref[batch, :, cols].astype(jnp.float32)
            stream[batch, :, cols] = added
            squares = squares + jnp.sum(added * added, axis=-1, keepdims=True)
        scale = lax.rsqrt(squares / width + 1e-06)
        gathered[batch, mine, core] = (stream[batch] * scale * gain_ref[...]).astype(jnp.bfloat16)
        for half in range(2):
            for way in range(2):
                ag_copy(way, 1, batch, mine, half).start()
            pair_copy(batch, mine, half).start()

    for load in loads[:2]:
        load.wait()

    @pl.loop(0, pieces)
    def _(piece):
        attend(0, piece)

        @pl.when(piece == pieces // 2 - 1)
        def _():
            pl.semaphore_wait(barrier, devices - 1)
            send_heads(0, 0)

    send_heads(0, 1)

    for load in loads[2:-2]:
        load.wait()
    ids = jnp.concatenate([ids_ref[batch] for batch in range(batches)], axis=1)
    gates = jnp.concatenate([gates_ref[batch] for batch in range(batches)], axis=1)
    gates = gates.astype(jnp.float32)
    gates = gates / jnp.sum(gates, axis=0, keepdims=True)
    for expert in range(devices):
        share_out[expert] = jnp.sum(jnp.where(ids == expert, gates, 0.0), axis=0, keepdims=True)
    share_in[me] = share_out[me]

    @pl.loop(1, devices)
    def _(k):
        share_copy((me + k) % devices).start()

    @pl.loop(0, pieces)
    def _(piece):
        attend(1, piece)

        @pl.when(piece == pieces // 2)
        def _():
            send_heads(1, 0)
            take_heads(0)

    send_heads(1, 1)

    shared().wait_recv()
    for load in loads[-2:]:
        load.wait()

    tile = 512

    def compute(blocks):
        for at, (batch, chip, which) in enumerate(blocks):
            xs[at * rows : (at + 1) * rows, :] = gathered[batch, chip, which]
            spread = jnp.broadcast_to(share_in[chip * 2 + which], (rows, share_in.shape[2]))
            lane = lax.broadcasted_iota(jnp.int32, spread.shape, 1)
            row = lax.broadcasted_iota(jnp.int32, spread.shape, 0)
            share = jnp.sum(
                jnp.where(lane == row + batch * rows, spread, 0.0), axis=-1, keepdims=True
            )
            sh[at * rows : (at + 1) * rows, :] = jnp.broadcast_to(share, spread.shape)
        taken = slice(0, len(blocks) * rows)
        gate = jnp.dot(xs[taken], gu[:, :hidden], preferred_element_type=jnp.float32)
        up = jnp.dot(xs[taken], gu[:, hidden:], preferred_element_type=jnp.float32)
        act[taken] = (gate / (1.0 + jnp.exp(-gate)) * up).astype(jnp.bfloat16)

        @pl.loop(0, width // tile)
        def _(j):
            cols = pl.ds(pl.multiple_of(j * tile, tile), tile)
            result = jnp.dot(act[taken], dn[:, cols], preferred_element_type=jnp.float32)
            for at, (batch, chip, which) in enumerate(blocks):
                share = sh[at * rows : (at + 1) * rows, :1]
                piece = result[at * rows : (at + 1) * rows]
                partial[batch, chip, which, :, cols] = (piece * share).astype(jnp.bfloat16)

    def gather_sum(batch, dest):
        return partial[batch, dest, core].astype(jnp.float32) + pairbuf[batch, dest].astype(
            jnp.float32
        )

    def around(dist):
        return chip_at(pos - dist), chip_at(pos + dist)

    def arrive(way, dist, batch, half):
        origin = around(dist)[way]
        ag_copy(way, dist, batch, origin, half).wait_recv()
        if isinstance(dist, int):
            if dist + 1 < far or (dist < far and batch == way):
                ag_copy(way, dist + 1, batch, origin, half).start()
        else:

            @pl.when((dist + 1 < far) | (batch == way))
            def _():
                ag_copy(way, dist + 1, batch, origin, half).start()

        pair_copy(batch, origin, half).start()

    def hand_on(dist, batch):
        for half in range(2):
            for way in range(2):
                arrive(way, dist, batch, half)

    def work(batch, origin):
        pair_arrival(batch, origin).wait_recv()
        compute([(batch, origin, which) for which in range(2)])
        sum_copy(batch, origin).start()

    def place(step):
        batch = (step + 1) % 2
        return batch, (step + 1) // 2 + 1 - batch

    def first(step):
        batch, dist = place(step)
        return batch, chip_at(pos - dist)

    def second(step):
        batch, dist = place(step)
        return batch, chip_at(pos + dist)

    def leaf(batch):
        way = 1 - batch
        dest = chip_at(pos + sign[way] * (far - 1))
        sum_copy(batch, dest).wait_recv()
        partial[batch, dest, core] = gather_sum(batch, dest).astype(jnp.bfloat16)
        rs_copy(way, 1, batch, dest).start()

    last = chip_at(pos + far)

    def turn_round(batch):
        sum_copy(batch, last).wait_recv()
        partial[batch, last, core] = gather_sum(batch, last).astype(jnp.bfloat16)
        rs_copy(batch, 0, batch, last).start()

    hand_on(1, 0)
    work(0, mine)
    take_heads(1)
    for origin in around(1):
        work(0, origin)

    @pl.loop(1, 2 * (far - 2) + 1)
    def _(step):
        batch, dist = place(step)
        hand_on(dist, batch)
        work(*second(step - 1))
        work(*first(step))

    for half in range(2):
        arrive(0, far, 0, half)
        arrive(1, far - 1, 1, half)
    work(0, last)
    leaf(0)
    turn_round(0)
    for half in range(2):
        arrive(0, far - 1, 1, half)
        arrive(1, far, 1, half)
    work(1, around(far - 1)[1])
    work(1, last)
    leaf(1)
    turn_round(1)

    def pass_on(way, turn, batch):
        dest = chip_at(pos + sign[way] * (far - turn))
        sum_copy(batch, dest).wait_recv()
        rs_copy(way, turn - 1, batch, dest).wait_recv()
        partial[batch, dest, core] = (
            gather_sum(batch, dest) + ringbuf[way, turn - 1, batch].astype(jnp.float32)
        ).astype(jnp.bfloat16)
        rs_copy(way, turn, batch, dest).start()

    pass_on(1, 2, 0)
    pass_on(0, 1, 0)
    work(*second(2 * (far - 2)))
    work(1, around(far - 1)[0])
    pass_on(0, 2, 1)
    pass_on(1, 1, 1)

    @pl.loop(2, far - 2)
    def _(turn):
        pass_on(1, turn + 1, 0)
        pass_on(0, turn, 0)
        pass_on(0, turn + 1, 1)
        pass_on(1, turn, 1)

    def pass_half(way, late, half):
        dest = chip_at(pos + sign[way] * (2 - late))
        some = halves[half]
        if late:
            half_copy(way, 0, half, dest).wait_recv()
        partial[way, dest, core, some] = (
            partial[way, dest, core, some].astype(jnp.float32)
            + pairbuf[way, dest, some].astype(jnp.float32)
            + ringbuf[way, far - 3 + late, way, some].astype(jnp.float32)
        ).astype(jnp.bfloat16)
        half_copy(way, late, half, dest).start()

    def pass_late(way):
        dest = chip_at(pos + sign[way] * 2)
        sum_copy(way, dest).wait_recv()
        rs_copy(way, far - 3, way, dest).wait_recv()
        for half in range(2):
            pass_half(way, 0, half)

    pass_on(1, far - 1, 0)
    pass_late(0)
    pass_on(0, far - 1, 1)
    pass_late(1)
    for way in range(2):
        sum_copy(way, chip_at(pos + sign[way])).wait_recv()

    for half in range(2):
        for way in range(2):
            pass_half(way, 1, half)

    shared().wait_send()
    for batch in range(batches):
        exchanged(batch).wait_send()
    some = gathered.at[0, pl.ds(0, chips - 1)]
    remote(some, some, ag_send, sh_recv, partner).wait_send()
    remote(gathered.at[0], gathered.at[0], agp_send, sh_recv, partner).wait_send()
    remote(partial.at[0], partial.at[0], rsp_send, sh_recv, partner).wait_send()

    for batch in range(batches):
        sum_copy(batch, mine).wait_recv()
        rs_copy(1 - batch, far - 1, batch, mine).wait_recv()
        stream[batch] = (
            stream[batch]
            + gather_sum(batch, mine)
            + ringbuf[1 - batch, far - 1, batch].astype(jnp.float32)
        )
    for half in range(2):
        some = halves[half]
        for batch in range(batches):
            half_copy(batch, 1, half, mine).wait_recv()
            out_ref[batch, some] = (
                stream[batch, some] + ringbuf[batch, far - 1, batch, some].astype(jnp.float32)
            ).astype(out_ref.dtype)
    some = partial.at[0, pl.ds(0, chips - 1)]
    remote(some, some, rs_send, sh_recv, partner).wait_send()


def fits(devices, rows, width, hidden):
    block = 2 * rows * (width + 128) * 2
    needed = 3 * devices * block + 3 * width * hidden * 2 + 8 * rows * width * 4
    return devices % 4 == 0 and 12 <= devices <= 64 and rows % 32 == 0 and 2 * rows % 128 == 0 and needed < 48 * 1024 * 1024


def routed_layer(queries, keys_values, residual, norm_gain, ids, gates, gate_up, down_proj, kv_heads, devices):
    batches, rows, width = residual.shape
    length, part = queries.shape[1:]
    span = length // devices
    hidden = down_proj.shape[1]
    chips = devices // 2
    far = chips // 2
    dma = pltpu.SemaphoreType.DMA
    vmem = pl.BlockSpec(memory_space=pltpu.VMEM)
    anywhere = pl.BlockSpec(memory_space=pl.ANY)
    kind = jnp.bfloat16
    return pl.pallas_call(
        functools.partial(moe_kernel, chips),
        out_shape=pltpu.VMEM((batches, rows, width), kind),
        in_specs=[anywhere] * 8,
        out_specs=vmem,
        scratch_shapes=[
            pltpu.VMEM(queries.shape, kind),
            pltpu.VMEM(keys_values.shape, kind),
            pltpu.VMEM(residual.shape, kind),
            pltpu.VMEM((1, width), jnp.float32),
            pltpu.VMEM((batches, ids.shape[2], rows), jnp.int32),
            pltpu.VMEM((batches, ids.shape[2], rows), jnp.int32),
            pltpu.VMEM((batches, devices, span, part), kind),
            pltpu.VMEM((batches, devices, span, part), kind),
            pltpu.VMEM((batches, rows, width), jnp.float32),
            pltpu.VMEM((batches, chips, 2, rows, width), kind),
            pltpu.VMEM((batches, chips, 2, rows, width), kind),
            pltpu.VMEM((batches, chips, rows, width), kind),
            pltpu.VMEM((2, far, batches, rows, width), kind),
            pltpu.VMEM((width, 2 * hidden), kind),
            pltpu.VMEM((hidden, width), kind),
            pltpu.VMEM((4 * rows, width), kind),
            pltpu.VMEM((4 * rows, batches * rows), jnp.float32),
            pltpu.VMEM((4 * rows, hidden), kind),
            pltpu.VMEM((devices, 1, batches * rows), jnp.float32),
            pltpu.VMEM((devices, 1, batches * rows), jnp.float32),
            dma((2 * batches + 6,)),
            dma, dma,
            dma((batches,)), dma((batches,)),
            dma, dma((2, far, batches, 2)),
            dma, dma((batches, chips)),
            dma, dma((batches, chips)),
            dma, dma((2, far, batches)),
            dma((2, 2, 2)),
        ],
        compiler_params=pltpu.CompilerParams(
            collective_id=0, has_side_effects=True, vmem_limit_bytes=56 * 1024 * 1024
        ),
    )(
        queries, keys_values, residual, norm_gain.reshape(1, width),
        jnp.transpose(ids, (0, 2, 1)), jnp.transpose(gates, (0, 2, 1)), gate_up, down_proj,
    )


def body(queries, keys_values, residual, norm_gain, gate_up, down_proj, expert_ids, expert_gates):
    devices = lax.axis_size("dev")
    me = lax.axis_index("dev")
    model_width = residual.shape[2]
    kv_heads = model_width // queries.shape[3]
    experts = devices * gate_up.shape[0]
    batches, unit, length, feat_width = queries.shape
    positions = length // devices
    if batches == 2 and fits(devices, residual.shape[1], model_width, down_proj.shape[1]):
        return routed_layer(
            queries[:, 0], keys_values[:, 0], residual, norm_gain, expert_ids, expert_gates,
            gate_up, down_proj, kv_heads, devices,
        )
    weights = dense_shares(expert_ids, expert_gates, experts)
    blended = attend_local(queries, keys_values)
    weights = lax.all_gather(weights, "dev", axis=1, tiled=True)
    mine = jnp.sum(
        jnp.where(jnp.arange(experts, dtype=jnp.int32) == me, weights, 0.0), axis=-1, keepdims=True
    )
    pieces = []
    for batch_index in range(batches):
        outgoing_rows = blended[batch_index].reshape(1, devices, positions, feat_width)
        arrived_rows = lax.all_to_all(outgoing_rows, "dev", split_axis=1, concat_axis=1, tiled=True)
        attn_rows = to_owners(arrived_rows, kv_heads)
        stream, normed = prepare(attn_rows[0], residual[batch_index], norm_gain)
        rows_in = lax.all_gather(normed, "dev", axis=0, tiled=True)
        partial = run_expert(rows_in, gate_up, down_proj, mine[batch_index])
        summed = lax.psum_scatter(partial, "dev", scatter_dimension=0, tiled=True)
        pieces.append((stream + summed.astype(jnp.float32)).astype(jnp.bfloat16))
    return jnp.stack(pieces, axis=0)


def solution(mesh):
    in_specs = (
        P(None, ("groups", "dev"), None, None),
        P(None, ("groups", "dev"), None, None, None),
        P(None, ("groups", "dev"), None),
        P(),
        P("dev", None, None),
        P("dev", None, None),
        P(None, ("groups", "dev"), None),
        P(None, ("groups", "dev"), None),
    )
    out_specs = P(None, ("groups", "dev"), None)
    return jax.shard_map(body, mesh=mesh, in_specs=in_specs, out_specs=out_specs, check_vma=False)
```

```python
import functools
import math

import jax
import jax.numpy as jnp
from jax import lax
from jax.experimental import pallas as pl
from jax.experimental.pallas import tpu as pltpu
from jax.sharding import PartitionSpec as P


def attend_pair(heads, pair_rows, keys, values):
    length = pair_rows.shape[0]
    context, head_size = keys.shape
    past = context - length
    query = jnp.concatenate(
        [pair_rows[:, head * head_size : (head + 1) * head_size] for head in range(heads)], axis=0
    )
    scores = lax.dot_general(
        query, keys, (((1,), (1,)), ((), ())), preferred_element_type=jnp.float32
    )
    rate = math.log2(math.e) / math.sqrt(head_size)
    old, new = scores[:, :past], scores[:, past:]
    row = lax.broadcasted_iota(jnp.int32, new.shape, 0) % length
    col = lax.broadcasted_iota(jnp.int32, new.shape, 1)
    new = jnp.where(col <= row, new, -1e30)
    highest = jnp.maximum(
        jnp.max(old, axis=-1, keepdims=True), jnp.max(new, axis=-1, keepdims=True)
    )
    old = jnp.exp2((old - highest) * rate)
    new = jnp.exp2((new - highest) * rate)
    totals = jnp.sum(old, axis=-1, keepdims=True) + jnp.sum(new, axis=-1, keepdims=True)
    blended = jnp.dot(
        old.astype(jnp.bfloat16), values[:past], preferred_element_type=jnp.float32
    ) + jnp.dot(new.astype(jnp.bfloat16), values[past:], preferred_element_type=jnp.float32)
    return blended * (1.0 / totals)


def attend_kernel(heads, q_ref, kv_ref, out_ref):
    length = q_ref.shape[1]
    head_size = kv_ref.shape[4]
    blended = attend_pair(heads, q_ref[0], kv_ref[0, 0, 0], kv_ref[0, 0, 1])
    for head in range(heads):
        out_ref[0, :, head * head_size : (head + 1) * head_size] = blended[
            head * length : (head + 1) * length
        ].astype(jnp.bfloat16)


def attend_local(queries, keys_values):
    batches, unit, length, feat_width = queries.shape
    context, head_size = keys_values.shape[3:]
    heads = 2
    wide = heads * head_size
    return pl.pallas_call(
        functools.partial(attend_kernel, heads),
        grid=(batches, feat_width // wide),
        out_shape=jax.ShapeDtypeStruct((batches, length, feat_width), jnp.bfloat16),
        in_specs=[
            pl.BlockSpec((1, length, wide), lambda b, h: (b, 0, h)),
            pl.BlockSpec((1, 1, 2, context, head_size), lambda b, h: (b, 0, 0, 0, 0)),
        ],
        out_specs=pl.BlockSpec((1, length, wide), lambda b, h: (b, 0, h)),
        compiler_params=pltpu.CompilerParams(vmem_limit_bytes=40 * 1024 * 1024),
    )(queries.reshape(batches, length, feat_width), keys_values)


def to_owners(exchanged, kv_heads):
    batches, sources, positions, feat_width = exchanged.shape
    grouped = exchanged.reshape(batches, sources // kv_heads, kv_heads, positions, feat_width)
    grouped = jnp.transpose(grouped, (0, 1, 3, 2, 4))
    return grouped.reshape(batches, sources // kv_heads * positions, kv_heads * feat_width)


def prepare(attn_rows, residual, norm_gain):
    stream = residual.astype(jnp.float32) + attn_rows.astype(jnp.float32)
    meansq = jnp.mean(stream * stream, axis=-1, keepdims=True)
    normed = (stream * lax.rsqrt(meansq + 1e-06) * norm_gain).astype(jnp.bfloat16)
    return stream, normed


def dense_shares(expert_ids, expert_gates, experts):
    shares = expert_gates.astype(jnp.float32)
    shares = shares / jnp.sum(shares, axis=-1, keepdims=True)
    named = expert_ids[..., None] == jnp.arange(experts, dtype=jnp.int32)
    return jnp.sum(jnp.where(named, shares[..., None], 0.0), axis=-2)


def run_expert(rows_in, gate_up, down_proj, weight):
    hidden_width = down_proj.shape[1]
    projected = jnp.dot(rows_in, gate_up[0], preferred_element_type=jnp.float32)
    hidden = (jax.nn.silu(projected[:, :hidden_width]) * projected[:, hidden_width:]).astype(
        jnp.bfloat16
    )
    output = jnp.dot(hidden, down_proj[0], preferred_element_type=jnp.float32)
    return (output * weight).astype(jnp.bfloat16)


MESH = pl.DeviceIdType.MESH


def moe_kernel(
    chips, q_hbm, kv_hbm, res_hbm, gain_hbm, ids_hbm, gates_hbm, gu_hbm, dn_hbm, out_ref,
    q_ref, kv_ref, res_ref, gain_ref, ids_ref, gates_ref,
    heads_ref, attn, stream, gathered, partial, pairbuf, ringbuf, gu, dn, xs, sh, act, share_out, share_in,
    load_sem, sh_send, sh_recv, ex_send, ex_recv, ag_send, ag_recv, agp_send, agp_recv, rsp_send, rsp_recv, rs_send, rs_recv,
    half_recv,
):
    batches, rows, width = res_ref.shape
    devices = 2 * chips
    part = attn.shape[3]
    kv_heads = width // part
    hidden = dn.shape[0]
    far = chips // 2
    me = lax.axis_index("dev")
    core = me % 2
    mine = me // 2
    odd = mine % 2
    pos = odd * ((mine + 1) // 2) + (1 - odd) * ((chips - mine // 2) % chips)

    def chip_at(place):
        q = (place + 2 * chips) % chips
        upper = q // (far + 1)
        some = (q + chips - 1) // chips
        return some * ((1 - upper) * (2 * q - 1) + upper * 2 * (chips - q))

    partner = mine * 2 + (1 - core)
    ahead = (chip_at(pos + 1) * 2 + core, chip_at(pos - 1) * 2 + core)
    sign = (1, -1)
    halves = (slice(0, rows // 2), slice(rows // 2, rows))

    def remote(src, dst, send, recv, target):
        return pltpu.make_async_remote_copy(
            src_ref=src, dst_ref=dst, send_sem=send, recv_sem=recv,
            device_id={"dev": target}, device_id_type=MESH,
        )

    side = devices // 2

    def own_first(chip, half):
        at = (chip // (chips // 2) + half) % 2
        return pl.ds(pl.multiple_of(at * (rows // 2), rows // 2), rows // 2)

    def ag_copy(way, dist, batch, origin, half):
        slot = gathered.at[batch, origin, core, own_first(origin, half)]
        return remote(slot, slot, ag_send, ag_recv.at[way, dist - 1, batch, half], ahead[way])

    def pair_copy(batch, origin, half):
        slot = gathered.at[batch, origin, core, own_first(origin, half)]
        return remote(slot, slot, agp_send, agp_recv.at[batch, origin], partner)

    def pair_arrival(batch, origin):
        slot = gathered.at[batch, origin, 1 - core]
        return remote(slot, slot, agp_send, agp_recv.at[batch, origin], partner)

    def sum_copy(batch, dest):
        return remote(
            partial.at[batch, dest, 1 - core], pairbuf.at[batch, dest],
            rsp_send, rsp_recv.at[batch, dest], partner,
        )

    def rs_copy(way, turn, batch, dest):
        return remote(
            partial.at[batch, dest, core], ringbuf.at[way, turn, batch],
            rs_send, rs_recv.at[way, turn, batch], ahead[way],
        )

    def half_copy(way, late, half, dest):
        turn, some = far - 2 + late, halves[half]
        return remote(
            partial.at[way, dest, core, some], ringbuf.at[way, turn, way, some],
            rs_send, half_recv.at[way, late, half], ahead[way],
        )

    def exchange(batch, target, cols, half):
        return remote(
            heads_ref.at[batch, target, :, cols], attn.at[batch, me, :, cols],
            ex_send.at[batch], ex_recv.at[batch, half], target,
        )

    def exchanged(batch, half, count):
        slots = attn.at[batch, pl.ds(0, count)]
        return remote(slots, slots, ex_send.at[batch], ex_recv.at[batch, half], partner)

    def share_copy(target):
        return remote(share_out.at[target], share_in.at[me], sh_send, sh_recv, target)

    def shared():
        slots = share_in.at[pl.ds(0, devices - 1)]
        return remote(slots, slots, sh_send, sh_recv, partner)

    barrier = pltpu.get_barrier_semaphore()

    @pl.loop(1, devices)
    def _(k):
        target = (me + k) % devices
        pl.semaphore_signal(barrier, inc=1, device_id={"dev": target}, device_id_type=MESH)

    pairs = [(q_hbm.at[0], q_ref.at[0]), (kv_hbm.at[0], kv_ref.at[0])]
    pairs += [(ids_hbm, ids_ref), (gates_hbm, gates_ref), (gain_hbm, gain_ref), (res_hbm, res_ref)]
    for batch in range(1, batches):
        pairs += [(q_hbm.at[batch], q_ref.at[batch]), (kv_hbm.at[batch], kv_ref.at[batch])]
    pairs += [(gu_hbm.at[0], gu), (dn_hbm.at[0], dn)]
    loads = [
        pltpu.make_async_copy(src, dst, load_sem.at[at]) for at, (src, dst) in enumerate(pairs)
    ]
    for load in loads[:2]:
        load.start()

    head_size = kv_ref.shape[3]
    length = q_ref.shape[1]

    wide = 2 * head_size
    pieces = part // wide

    def columns(piece):
        return pl.ds(pl.multiple_of(piece * wide, wide), wide)

    def attend(batch, piece):
        cols = columns(piece)
        blended = attend_pair(2, q_ref[batch, :, cols], kv_ref[batch, 0], kv_ref[batch, 1])
        for head in range(2):
            at = pl.ds(pl.multiple_of(piece * wide + head * head_size, head_size), head_size)
            heads_ref[batch, :, :, at] = blended[head * length : (head + 1) * length].reshape(
                devices, length // devices, head_size
            ).astype(jnp.bfloat16)

    def send_heads(batch, portion):
        cols = slice(portion * part // 2, (portion + 1) * part // 2)

        @pl.loop(1, side)
        def _(k):
            exchange(batch, me // side * side + (me + k) % side, cols, 0).start()

        @pl.loop(0, side)
        def _(k):
            exchange(batch, (1 - me // side) * side + (me + k) % side, cols, 1).start()

    def take_heads(batch, half):
        if half == 0:
            attn[batch, me] = heads_ref[batch, me]
        exchanged(batch, half, side - 1 + half).wait_recv()
        some = own_first(mine, half)
        first_slot = pl.multiple_of((mine // (chips // 2) + half) % 2 * side, side)
        arrived = attn[batch, pl.ds(first_slot, side)]
        arrived = arrived.reshape(side // kv_heads, kv_heads, rows * kv_heads // devices, part)
        squares = jnp.zeros((rows // 2, 1), jnp.float32)
        for head in range(kv_heads):
            cols = slice(head * part, (head + 1) * part)
            added = arrived[:, head].astype(jnp.float32).reshape(rows // 2, part)
            added = added + res_ref[batch, some, cols].astype(jnp.float32)
            stream[batch, some, cols] = added
            squares = squares + jnp.sum(added * added, axis=-1, keepdims=True)
        scale = lax.rsqrt(squares / width + 1e-06)
        gathered[batch, mine, core, some] = (stream[batch, some] * scale * gain_ref[...]).astype(
            jnp.bfloat16
        )
        for way in range(2):
            ag_copy(way, 1, batch, mine, half).start()
        pair_copy(batch, mine, half).start()

    for load in loads[:2]:
        load.wait()
    for load in loads[2:]:
        load.start()

    @pl.loop(0, pieces)
    def _(piece):
        attend(0, piece)

        @pl.when(piece == pieces // 2 - 1)
        def _():
            pl.semaphore_wait(barrier, devices - 1)
            send_heads(0, 0)

    send_heads(0, 1)

    for load in loads[2:-2]:
        load.wait()
    ids = jnp.concatenate([ids_ref[batch] for batch in range(batches)], axis=1)
    gates = jnp.concatenate([gates_ref[batch] for batch in range(batches)], axis=1)
    gates = gates.astype(jnp.float32)
    gates = gates / jnp.sum(gates, axis=0, keepdims=True)
    for expert in range(devices):
        share_out[expert] = jnp.sum(jnp.where(ids == expert, gates, 0.0), axis=0, keepdims=True)
    share_in[me] = share_out[me]

    @pl.loop(1, devices)
    def _(k):
        share_copy((me + k) % devices).start()

    @pl.loop(0, pieces)
    def _(piece):
        attend(1, piece)

        @pl.when(piece == pieces // 2)
        def _():
            send_heads(1, 0)
            take_heads(0, 0)

    take_heads(0, 1)
    send_heads(1, 1)

    shared().wait_recv()
    for load in loads[-2:]:
        load.wait()

    tile = 512

    def compute(blocks):
        for at, (batch, chip, which) in enumerate(blocks):
            xs[at * rows : (at + 1) * rows, :] = gathered[batch, chip, which]
            spread = jnp.broadcast_to(share_in[chip * 2 + which], (rows, share_in.shape[2]))
            lane = lax.broadcasted_iota(jnp.int32, spread.shape, 1)
            row = lax.broadcasted_iota(jnp.int32, spread.shape, 0)
            share = jnp.sum(
                jnp.where(lane == row + batch * rows, spread, 0.0), axis=-1, keepdims=True
            )
            sh[at * rows : (at + 1) * rows, :] = jnp.broadcast_to(share, spread.shape)
        taken = slice(0, len(blocks) * rows)
        gate = jnp.dot(xs[taken], gu[:, :hidden], preferred_element_type=jnp.float32)
        up = jnp.dot(xs[taken], gu[:, hidden:], preferred_element_type=jnp.float32)
        act[taken] = (gate / (1.0 + jnp.exp(-gate)) * up).astype(jnp.bfloat16)

        @pl.loop(0, width // tile)
        def _(j):
            cols = pl.ds(pl.multiple_of(j * tile, tile), tile)
            result = jnp.dot(act[taken], dn[:, cols], preferred_element_type=jnp.float32)
            for at, (batch, chip, which) in enumerate(blocks):
                share = sh[at * rows : (at + 1) * rows, :1]
                piece = result[at * rows : (at + 1) * rows]
                partial[batch, chip, which, :, cols] = (piece * share).astype(jnp.bfloat16)

    def gather_sum(batch, dest):
        return partial[batch, dest, core].astype(jnp.float32) + pairbuf[batch, dest].astype(
            jnp.float32
        )

    def around(dist):
        return chip_at(pos - dist), chip_at(pos + dist)

    def arrive(way, dist, batch, half):
        origin = around(dist)[way]
        ag_copy(way, dist, batch, origin, half).wait_recv()
        if dist < far and batch == way:
            ag_copy(way, dist + 1, batch, origin, half).start()
        pair_copy(batch, origin, half).start()

    short = chip_at(9 - pos) * 2 + core
    crosses = (pos % 4 // 2 * (1 - pos % 2), pos % 4 // 2 * (pos % 2))

    def hand_on(dist, batch):
        origins = around(dist)
        for half in range(2):
            for way in range(2):
                ag_copy(way, dist, batch, origins[way], half).wait_recv()
            for way in range(2):
                turned = crosses[way] * ((dist + 1) % 2)
                origin = origins[way] + turned * (origins[1 - way] - origins[way])
                target = ahead[way] + turned * (short - ahead[way])

                @pl.when((dist + 1 < far) | (batch == way))
                def _():
                    slot = gathered.at[batch, origin, core, own_first(origin, half)]
                    remote(slot, slot, ag_send, ag_recv.at[way, dist, batch, half], target).start()

            for way in range(2):
                pair_copy(batch, origins[way], half).start()

    def work(batch, origin):
        pair_arrival(batch, origin).wait_recv()
        compute([(batch, origin, which) for which in range(2)])
        sum_copy(batch, origin).start()

    def place(step):
        batch = (step + 1) % 2
        return batch, (step + 1) // 2 + 1 - batch

    def first(step):
        batch, dist = place(step)
        return batch, chip_at(pos - dist)

    def second(step):
        batch, dist = place(step)
        return batch, chip_at(pos + dist)

    def leaf(batch):
        way = 1 - batch
        dest = chip_at(pos + sign[way] * (far - 1))
        sum_copy(batch, dest).wait_recv()
        partial[batch, dest, core] = gather_sum(batch, dest).astype(jnp.bfloat16)
        rs_copy(way, 1, batch, dest).start()

    last = chip_at(pos + far)

    def turn_round(batch):
        sum_copy(batch, last).wait_recv()
        partial[batch, last, core] = gather_sum(batch, last).astype(jnp.bfloat16)
        rs_copy(batch, 0, batch, last).start()

    hand_on(1, 0)
    work(0, mine)
    for half in range(2):
        take_heads(1, half)
    for origin in around(1):
        work(0, origin)

    @pl.loop(1, 2 * (far - 2) + 1)
    def _(step):
        batch, dist = place(step)
        hand_on(dist, batch)
        work(*second(step - 1))
        work(*first(step))

    for half in range(2):
        arrive(0, far, 0, half)
        arrive(1, far - 1, 1, half)
    work(0, last)
    leaf(0)
    turn_round(0)
    for half in range(2):
        arrive(0, far - 1, 1, half)
        arrive(1, far, 1, half)
    work(1, around(far - 1)[1])
    work(1, last)
    leaf(1)
    turn_round(1)

    def pass_on(way, turn, batch):
        dest = chip_at(pos + sign[way] * (far - turn))
        sum_copy(batch, dest).wait_recv()
        rs_copy(way, turn - 1, batch, dest).wait_recv()
        partial[batch, dest, core] = (
            gather_sum(batch, dest) + ringbuf[way, turn - 1, batch].astype(jnp.float32)
        ).astype(jnp.bfloat16)
        rs_copy(way, turn, batch, dest).start()

    pass_on(1, 2, 0)
    pass_on(0, 1, 0)
    work(*second(2 * (far - 2)))
    work(1, around(far - 1)[0])
    pass_on(0, 2, 1)
    pass_on(1, 1, 1)

    @pl.loop(2, far - 2)
    def _(turn):
        pass_on(1, turn + 1, 0)
        pass_on(0, turn, 0)
        pass_on(0, turn + 1, 1)
        pass_on(1, turn, 1)

    def pass_half(way, late, half):
        dest = chip_at(pos + sign[way] * (2 - late))
        some = halves[half]
        if late:
            half_copy(way, 0, half, dest).wait_recv()
        partial[way, dest, core, some] = (
            partial[way, dest, core, some].astype(jnp.float32)
            + pairbuf[way, dest, some].astype(jnp.float32)
            + ringbuf[way, far - 3 + late, way, some].astype(jnp.float32)
        ).astype(jnp.bfloat16)
        half_copy(way, late, half, dest).start()

    def pass_late(way):
        dest = chip_at(pos + sign[way] * 2)
        sum_copy(way, dest).wait_recv()
        rs_copy(way, far - 3, way, dest).wait_recv()
        for half in range(2):
            pass_half(way, 0, half)

    pass_on(1, far - 1, 0)
    pass_late(0)
    pass_on(0, far - 1, 1)
    pass_late(1)
    for way in range(2):
        sum_copy(way, chip_at(pos + sign[way])).wait_recv()

    for half in range(2):
        for way in range(2):
            pass_half(way, 1, half)

    shared().wait_send()
    for batch in range(batches):
        exchanged(batch, 0, devices - 1).wait_send()
    some = gathered.at[0, pl.ds(0, chips - 1)]
    remote(some, some, ag_send, sh_recv, partner).wait_send()
    remote(gathered.at[0], gathered.at[0], agp_send, sh_recv, partner).wait_send()
    remote(partial.at[0], partial.at[0], rsp_send, sh_recv, partner).wait_send()

    for batch in range(batches):
        sum_copy(batch, mine).wait_recv()
        rs_copy(1 - batch, far - 1, batch, mine).wait_recv()
        stream[batch] = (
            stream[batch]
            + gather_sum(batch, mine)
            + ringbuf[1 - batch, far - 1, batch].astype(jnp.float32)
        )
    for half in range(2):
        some = halves[half]
        for batch in range(batches):
            half_copy(batch, 1, half, mine).wait_recv()
            out_ref[batch, some] = (
                stream[batch, some] + ringbuf[batch, far - 1, batch, some].astype(jnp.float32)
            ).astype(out_ref.dtype)
    some = partial.at[0, pl.ds(0, chips - 1)]
    remote(some, some, rs_send, sh_recv, partner).wait_send()


def fits(devices, rows, width, hidden):
    block = 2 * rows * (width + 128) * 2
    needed = 3 * devices * block + 3 * width * hidden * 2 + 8 * rows * width * 4
    return devices % 4 == 0 and devices == 2 * 8 and rows % 32 == 0 and 2 * rows % 128 == 0 and needed < 48 * 1024 * 1024


def routed_layer(queries, keys_values, residual, norm_gain, ids, gates, gate_up, down_proj, kv_heads, devices):
    batches, rows, width = residual.shape
    length, part = queries.shape[1:]
    span = length // devices
    hidden = down_proj.shape[1]
    chips = devices // 2
    far = chips // 2
    dma = pltpu.SemaphoreType.DMA
    vmem = pl.BlockSpec(memory_space=pltpu.VMEM)
    anywhere = pl.BlockSpec(memory_space=pl.ANY)
    kind = jnp.bfloat16
    return pl.pallas_call(
        functools.partial(moe_kernel, chips),
        out_shape=pltpu.VMEM((batches, rows, width), kind),
        in_specs=[anywhere] * 8,
        out_specs=vmem,
        scratch_shapes=[
            pltpu.VMEM(queries.shape, kind),
            pltpu.VMEM(keys_values.shape, kind),
            pltpu.VMEM(residual.shape, kind),
            pltpu.VMEM((1, width), jnp.float32),
            pltpu.VMEM((batches, ids.shape[2], rows), jnp.int32),
            pltpu.VMEM((batches, ids.shape[2], rows), jnp.int32),
            pltpu.VMEM((batches, devices, span, part), kind),
            pltpu.VMEM((batches, devices, span, part), kind),
            pltpu.VMEM((batches, rows, width), jnp.float32),
            pltpu.VMEM((batches, chips, 2, rows, width), kind),
            pltpu.VMEM((batches, chips, 2, rows, width), kind),
            pltpu.VMEM((batches, chips, rows, width), kind),
            pltpu.VMEM((2, far, batches, rows, width), kind),
            pltpu.VMEM((width, 2 * hidden), kind),
            pltpu.VMEM((hidden, width), kind),
            pltpu.VMEM((4 * rows, width), kind),
            pltpu.VMEM((4 * rows, batches * rows), jnp.float32),
            pltpu.VMEM((4 * rows, hidden), kind),
            pltpu.VMEM((devices, 1, batches * rows), jnp.float32),
            pltpu.VMEM((devices, 1, batches * rows), jnp.float32),
            dma((2 * batches + 6,)),
            dma, dma,
            dma((batches,)), dma((batches, 2)),
            dma, dma((2, far, batches, 2)),
            dma, dma((batches, chips)),
            dma, dma((batches, chips)),
            dma, dma((2, far, batches)),
            dma((2, 2, 2)),
        ],
        compiler_params=pltpu.CompilerParams(
            collective_id=0, has_side_effects=True, vmem_limit_bytes=56 * 1024 * 1024
        ),
    )(
        queries, keys_values, residual, norm_gain.reshape(1, width),
        jnp.transpose(ids, (0, 2, 1)), jnp.transpose(gates, (0, 2, 1)), gate_up, down_proj,
    )


def body(queries, keys_values, residual, norm_gain, gate_up, down_proj, expert_ids, expert_gates):
    devices = lax.axis_size("dev")
    me = lax.axis_index("dev")
    model_width = residual.shape[2]
    kv_heads = model_width // queries.shape[3]
    experts = devices * gate_up.shape[0]
    batches, unit, length, feat_width = queries.shape
    positions = length // devices
    if batches == 2 and fits(devices, residual.shape[1], model_width, down_proj.shape[1]):
        return routed_layer(
            queries[:, 0], keys_values[:, 0], residual, norm_gain, expert_ids, expert_gates,
            gate_up, down_proj, kv_heads, devices,
        )
    weights = dense_shares(expert_ids, expert_gates, experts)
    blended = attend_local(queries, keys_values)
    weights = lax.all_gather(weights, "dev", axis=1, tiled=True)
    mine = jnp.sum(
        jnp.where(jnp.arange(experts, dtype=jnp.int32) == me, weights, 0.0), axis=-1, keepdims=True
    )
    pieces = []
    for batch_index in range(batches):
        outgoing_rows = blended[batch_index].reshape(1, devices, positions, feat_width)
        arrived_rows = lax.all_to_all(outgoing_rows, "dev", split_axis=1, concat_axis=1, tiled=True)
        attn_rows = to_owners(arrived_rows, kv_heads)
        stream, normed = prepare(attn_rows[0], residual[batch_index], norm_gain)
        rows_in = lax.all_gather(normed, "dev", axis=0, tiled=True)
        partial = run_expert(rows_in, gate_up, down_proj, mine[batch_index])
        summed = lax.psum_scatter(partial, "dev", scatter_dimension=0, tiled=True)
        pieces.append((stream + summed.astype(jnp.float32)).astype(jnp.bfloat16))
    return jnp.stack(pieces, axis=0)


def solution(mesh):
    in_specs = (
        P(None, ("groups", "dev"), None, None),
        P(None, ("groups", "dev"), None, None, None),
        P(None, ("groups", "dev"), None),
        P(),
        P("dev", None, None),
        P("dev", None, None),
        P(None, ("groups", "dev"), None),
        P(None, ("groups", "dev"), None),
    )
    out_specs = P(None, ("groups", "dev"), None)
    return jax.shard_map(body, mesh=mesh, in_specs=in_specs, out_specs=out_specs, check_vma=False)
```

```python
import functools
import math

import jax
import jax.numpy as jnp
from jax import lax
from jax.experimental import pallas as pl
from jax.experimental.pallas import tpu as pltpu
from jax.sharding import PartitionSpec as P


def attend_pair(heads, pair_rows, keys, values):
    length = pair_rows.shape[0]
    context, head_size = keys.shape
    past = context - length
    query = jnp.concatenate(
        [pair_rows[:, head * head_size : (head + 1) * head_size] for head in range(heads)], axis=0
    )
    scores = lax.dot_general(
        query, keys, (((1,), (1,)), ((), ())), preferred_element_type=jnp.float32
    )
    rate = math.log2(math.e) / math.sqrt(head_size)
    old, new = scores[:, :past], scores[:, past:]
    row = lax.broadcasted_iota(jnp.int32, new.shape, 0) % length
    col = lax.broadcasted_iota(jnp.int32, new.shape, 1)
    new = jnp.where(col <= row, new, -1e30)
    highest = jnp.maximum(
        jnp.max(old, axis=-1, keepdims=True), jnp.max(new, axis=-1, keepdims=True)
    )
    old = jnp.exp2((old - highest) * rate)
    new = jnp.exp2((new - highest) * rate)
    totals = jnp.sum(old, axis=-1, keepdims=True) + jnp.sum(new, axis=-1, keepdims=True)
    blended = jnp.dot(
        old.astype(jnp.bfloat16), values[:past], preferred_element_type=jnp.float32
    ) + jnp.dot(new.astype(jnp.bfloat16), values[past:], preferred_element_type=jnp.float32)
    return blended * (1.0 / totals)


def attend_kernel(heads, q_ref, kv_ref, out_ref):
    length = q_ref.shape[1]
    head_size = kv_ref.shape[4]
    blended = attend_pair(heads, q_ref[0], kv_ref[0, 0, 0], kv_ref[0, 0, 1])
    for head in range(heads):
        out_ref[0, :, head * head_size : (head + 1) * head_size] = blended[
            head * length : (head + 1) * length
        ].astype(jnp.bfloat16)


def attend_local(queries, keys_values):
    batches, unit, length, feat_width = queries.shape
    context, head_size = keys_values.shape[3:]
    heads = 2
    wide = heads * head_size
    return pl.pallas_call(
        functools.partial(attend_kernel, heads),
        grid=(batches, feat_width // wide),
        out_shape=jax.ShapeDtypeStruct((batches, length, feat_width), jnp.bfloat16),
        in_specs=[
            pl.BlockSpec((1, length, wide), lambda b, h: (b, 0, h)),
            pl.BlockSpec((1, 1, 2, context, head_size), lambda b, h: (b, 0, 0, 0, 0)),
        ],
        out_specs=pl.BlockSpec((1, length, wide), lambda b, h: (b, 0, h)),
        compiler_params=pltpu.CompilerParams(vmem_limit_bytes=40 * 1024 * 1024),
    )(queries.reshape(batches, length, feat_width), keys_values)


def to_owners(exchanged, kv_heads):
    batches, sources, positions, feat_width = exchanged.shape
    grouped = exchanged.reshape(batches, sources // kv_heads, kv_heads, positions, feat_width)
    grouped = jnp.transpose(grouped, (0, 1, 3, 2, 4))
    return grouped.reshape(batches, sources // kv_heads * positions, kv_heads * feat_width)


def prepare(attn_rows, residual, norm_gain):
    stream = residual.astype(jnp.float32) + attn_rows.astype(jnp.float32)
    meansq = jnp.mean(stream * stream, axis=-1, keepdims=True)
    normed = (stream * lax.rsqrt(meansq + 1e-06) * norm_gain).astype(jnp.bfloat16)
    return stream, normed


def dense_shares(expert_ids, expert_gates, experts):
    shares = expert_gates.astype(jnp.float32)
    shares = shares / jnp.sum(shares, axis=-1, keepdims=True)
    named = expert_ids[..., None] == jnp.arange(experts, dtype=jnp.int32)
    return jnp.sum(jnp.where(named, shares[..., None], 0.0), axis=-2)


def run_expert(rows_in, gate_up, down_proj, weight):
    hidden_width = down_proj.shape[1]
    projected = jnp.dot(rows_in, gate_up[0], preferred_element_type=jnp.float32)
    hidden = (jax.nn.silu(projected[:, :hidden_width]) * projected[:, hidden_width:]).astype(
        jnp.bfloat16
    )
    output = jnp.dot(hidden, down_proj[0], preferred_element_type=jnp.float32)
    return (output * weight).astype(jnp.bfloat16)


MESH = pl.DeviceIdType.MESH


def moe_kernel(
    chips, q_hbm, kv_hbm, res_hbm, gain_hbm, ids_hbm, gates_hbm, gu_hbm, dn_hbm, out_ref,
    q_ref, kv_ref, res_ref, gain_ref, ids_ref, gates_ref,
    heads_ref, attn, stream, gathered, partial, pairbuf, ringbuf, gu, dn, xs, sh, act, share_out, share_in,
    load_sem, sh_send, sh_recv, ex_send, ex_recv, ag_send, ag_recv, agp_send, agp_recv, rsp_send, rsp_recv, rs_send, rs_recv,
    half_recv,
):
    batches, rows, width = res_ref.shape
    devices = 2 * chips
    part = attn.shape[3]
    kv_heads = width // part
    hidden = dn.shape[0]
    far = chips // 2
    me = lax.axis_index("dev")
    core = me % 2
    mine = me // 2
    odd = mine % 2
    pos = odd * ((mine + 1) // 2) + (1 - odd) * ((chips - mine // 2) % chips)

    def chip_at(place):
        q = (place + 2 * chips) % chips
        upper = q // (far + 1)
        some = (q + chips - 1) // chips
        return some * ((1 - upper) * (2 * q - 1) + upper * 2 * (chips - q))

    partner = mine * 2 + (1 - core)
    ahead = (chip_at(pos + 1) * 2 + core, chip_at(pos - 1) * 2 + core)
    sign = (1, -1)
    halves = (slice(0, rows // 2), slice(rows // 2, rows))

    def remote(src, dst, send, recv, target):
        return pltpu.make_async_remote_copy(
            src_ref=src, dst_ref=dst, send_sem=send, recv_sem=recv,
            device_id={"dev": target}, device_id_type=MESH,
        )

    side = devices // 2

    def own_first(chip, half):
        at = (chip // (chips // 2) + half) % 2
        return pl.ds(pl.multiple_of(at * (rows // 2), rows // 2), rows // 2)

    def ag_copy(way, dist, batch, origin, half):
        slot = gathered.at[batch, origin, core, own_first(origin, half)]
        return remote(slot, slot, ag_send, ag_recv.at[way, dist - 1, batch, half], ahead[way])

    def pair_copy(batch, origin, half):
        slot = gathered.at[batch, origin, core, own_first(origin, half)]
        return remote(slot, slot, agp_send, agp_recv.at[batch, origin], partner)

    def pair_arrival(batch, origin):
        slot = gathered.at[batch, origin, 1 - core]
        return remote(slot, slot, agp_send, agp_recv.at[batch, origin], partner)

    def sum_copy(batch, dest):
        return remote(
            partial.at[batch, dest, 1 - core], pairbuf.at[batch, dest],
            rsp_send, rsp_recv.at[batch, dest], partner,
        )

    def rs_copy(way, turn, batch, dest):
        return remote(
            partial.at[batch, dest, core], ringbuf.at[way, turn, batch],
            rs_send, rs_recv.at[way, turn, batch], ahead[way],
        )

    def half_copy(way, late, half, dest):
        turn, some = far - 2 + late, halves[half]
        return remote(
            partial.at[way, dest, core, some], ringbuf.at[way, turn, way, some],
            rs_send, half_recv.at[way, late, half], ahead[way],
        )

    def exchange(batch, target, cols, half):
        return remote(
            heads_ref.at[batch, target, :, cols], attn.at[batch, me, :, cols],
            ex_send.at[batch], ex_recv.at[batch, half], target,
        )

    def exchanged(batch, half, count):
        slots = attn.at[batch, pl.ds(0, count)]
        return remote(slots, slots, ex_send.at[batch], ex_recv.at[batch, half], partner)

    def share_copy(target):
        return remote(share_out.at[target], share_in.at[me], sh_send, sh_recv, target)

    def shared():
        slots = share_in.at[pl.ds(0, devices - 1)]
        return remote(slots, slots, sh_send, sh_recv, partner)

    barrier = pltpu.get_barrier_semaphore()

    @pl.loop(1, devices)
    def _(k):
        target = (me + k) % devices
        pl.semaphore_signal(barrier, inc=1, device_id={"dev": target}, device_id_type=MESH)

    pairs = [(q_hbm.at[0], q_ref.at[0]), (kv_hbm.at[0], kv_ref.at[0])]
    pairs += [(ids_hbm, ids_ref), (gates_hbm, gates_ref), (gain_hbm, gain_ref), (res_hbm, res_ref)]
    for batch in range(1, batches):
        pairs += [(q_hbm.at[batch], q_ref.at[batch]), (kv_hbm.at[batch], kv_ref.at[batch])]
    pairs += [(gu_hbm.at[0], gu), (dn_hbm.at[0], dn)]
    loads = [
        pltpu.make_async_copy(src, dst, load_sem.at[at]) for at, (src, dst) in enumerate(pairs)
    ]
    for load in loads[:2]:
        load.start()

    head_size = kv_ref.shape[3]
    length = q_ref.shape[1]

    wide = 2 * head_size
    pieces = part // wide

    def columns(piece):
        return pl.ds(pl.multiple_of(piece * wide, wide), wide)

    def attend(batch, piece):
        cols = columns(piece)
        blended = attend_pair(2, q_ref[batch, :, cols], kv_ref[batch, 0], kv_ref[batch, 1])
        for head in range(2):
            at = pl.ds(pl.multiple_of(piece * wide + head * head_size, head_size), head_size)
            heads_ref[batch, :, :, at] = blended[head * length : (head + 1) * length].reshape(
                devices, length // devices, head_size
            ).astype(jnp.bfloat16)

    def send_heads(batch, portion):
        cols = slice(portion * part // 2, (portion + 1) * part // 2)

        @pl.loop(1, side)
        def _(k):
            exchange(batch, me // side * side + (me + k) % side, cols, 0).start()

        @pl.loop(0, side)
        def _(k):
            exchange(batch, (1 - me // side) * side + (me + k) % side, cols, 1).start()

    def take_heads(batch, half):
        if half == 0:
            attn[batch, me] = heads_ref[batch, me]
        exchanged(batch, half, side - 1 + half).wait_recv()
        some = own_first(mine, half)
        first_slot = pl.multiple_of((mine // (chips // 2) + half) % 2 * side, side)
        arrived = attn[batch, pl.ds(first_slot, side)]
        arrived = arrived.reshape(side // kv_heads, kv_heads, rows * kv_heads // devices, part)
        squares = jnp.zeros((rows // 2, 1), jnp.float32)
        for head in range(kv_heads):
            cols = slice(head * part, (head + 1) * part)
            added = arrived[:, head].astype(jnp.float32).reshape(rows // 2, part)
            added = added + res_ref[batch, some, cols].astype(jnp.float32)
            stream[batch, some, cols] = added
            squares = squares + jnp.sum(added * added, axis=-1, keepdims=True)
        scale = lax.rsqrt(squares / width + 1e-06)
        gathered[batch, mine, core, some] = (stream[batch, some] * scale * gain_ref[...]).astype(
            jnp.bfloat16
        )
        for way in range(2):
            ag_copy(way, 1, batch, mine, half).start()
        pair_copy(batch, mine, half).start()

    for load in loads[:2]:
        load.wait()
    for load in loads[2:]:
        load.start()

    @pl.loop(0, pieces)
    def _(piece):
        attend(0, piece)

        @pl.when(piece == pieces // 2 - 1)
        def _():
            pl.semaphore_wait(barrier, devices - 1)
            send_heads(0, 0)

    send_heads(0, 1)

    for load in loads[2:-2]:
        load.wait()
    ids = jnp.concatenate([ids_ref[batch] for batch in range(batches)], axis=1)
    gates = jnp.concatenate([gates_ref[batch] for batch in range(batches)], axis=1)
    gates = gates.astype(jnp.float32)
    gates = gates / jnp.sum(gates, axis=0, keepdims=True)
    for expert in range(devices):
        share_out[expert] = jnp.sum(jnp.where(ids == expert, gates, 0.0), axis=0, keepdims=True)
    share_in[me] = share_out[me]

    @pl.loop(1, devices)
    def _(k):
        share_copy((me + k) % devices).start()

    @pl.loop(0, pieces)
    def _(piece):
        attend(1, piece)

        @pl.when(piece == pieces // 2)
        def _():
            send_heads(1, 0)
            take_heads(0, 0)

    take_heads(0, 1)
    send_heads(1, 1)

    shared().wait_recv()
    for load in loads[-2:]:
        load.wait()

    tile = width // 2

    def compute(blocks):
        for at, (batch, chip, which) in enumerate(blocks):
            xs[at * rows : (at + 1) * rows, :] = gathered[batch, chip, which]
            spread = jnp.broadcast_to(share_in[chip * 2 + which], (rows, share_in.shape[2]))
            lane = lax.broadcasted_iota(jnp.int32, spread.shape, 1)
            row = lax.broadcasted_iota(jnp.int32, spread.shape, 0)
            share = jnp.sum(
                jnp.where(lane == row + batch * rows, spread, 0.0), axis=-1, keepdims=True
            )
            sh[at * rows : (at + 1) * rows, :] = jnp.broadcast_to(share, spread.shape)
        taken = slice(0, len(blocks) * rows)
        gate = jnp.dot(xs[taken], gu[:, :hidden], preferred_element_type=jnp.float32)
        up = jnp.dot(xs[taken], gu[:, hidden:], preferred_element_type=jnp.float32)
        act[taken] = (gate / (1.0 + jnp.exp(-gate)) * up).astype(jnp.bfloat16)

        @pl.loop(0, width // tile)
        def _(j):
            cols = pl.ds(pl.multiple_of(j * tile, tile), tile)
            result = jnp.dot(act[taken], dn[:, cols], preferred_element_type=jnp.float32)
            for at, (batch, chip, which) in enumerate(blocks):
                share = sh[at * rows : (at + 1) * rows, :1]
                piece = result[at * rows : (at + 1) * rows]
                partial[batch, chip, which, :, cols] = (piece * share).astype(jnp.bfloat16)

    def gather_sum(batch, dest):
        return partial[batch, dest, core].astype(jnp.float32) + pairbuf[batch, dest].astype(
            jnp.float32
        )

    def around(dist):
        return chip_at(pos - dist), chip_at(pos + dist)

    def arrive(way, dist, batch, half):
        origin = around(dist)[way]
        ag_copy(way, dist, batch, origin, half).wait_recv()
        if dist < far and batch == way:
            ag_copy(way, dist + 1, batch, origin, half).start()
        pair_copy(batch, origin, half).start()

    short = chip_at(9 - pos) * 2 + core
    crosses = (pos % 4 // 2 * (1 - pos % 2), pos % 4 // 2 * (pos % 2))

    def hand_on(dist, batch):
        origins = around(dist)
        for half in range(2):
            for way in range(2):
                ag_copy(way, dist, batch, origins[way], half).wait_recv()
            for way in range(2):
                turned = crosses[way] * ((dist + 1) % 2)
                origin = origins[way] + turned * (origins[1 - way] - origins[way])
                target = ahead[way] + turned * (short - ahead[way])

                @pl.when((dist + 1 < far) | (batch == way))
                def _():
                    slot = gathered.at[batch, origin, core, own_first(origin, half)]
                    remote(slot, slot, ag_send, ag_recv.at[way, dist, batch, half], target).start()

            for way in range(2):
                pair_copy(batch, origins[way], half).start()

    def work(batch, origin):
        pair_arrival(batch, origin).wait_recv()
        compute([(batch, origin, which) for which in range(2)])
        sum_copy(batch, origin).start()

    def place(step):
        batch = (step + 1) % 2
        return batch, (step + 1) // 2 + 1 - batch

    def first(step):
        batch, dist = place(step)
        return batch, chip_at(pos - dist)

    def second(step):
        batch, dist = place(step)
        return batch, chip_at(pos + dist)

    def leaf(batch):
        way = 1 - batch
        dest = chip_at(pos + sign[way] * (far - 1))
        sum_copy(batch, dest).wait_recv()
        partial[batch, dest, core] = gather_sum(batch, dest).astype(jnp.bfloat16)
        rs_copy(way, 1, batch, dest).start()

    last = chip_at(pos + far)

    def turn_round(batch):
        sum_copy(batch, last).wait_recv()
        partial[batch, last, core] = gather_sum(batch, last).astype(jnp.bfloat16)
        rs_copy(batch, 0, batch, last).start()

    hand_on(1, 0)
    work(0, mine)
    for half in range(2):
        take_heads(1, half)
    for origin in around(1):
        work(0, origin)

    @pl.loop(1, 2 * (far - 2) + 1)
    def _(step):
        batch, dist = place(step)
        hand_on(dist, batch)
        work(*second(step - 1))
        work(*first(step))

    for half in range(2):
        arrive(0, far, 0, half)
        arrive(1, far - 1, 1, half)
    work(0, last)
    leaf(0)
    turn_round(0)
    for half in range(2):
        arrive(0, far - 1, 1, half)
        arrive(1, far, 1, half)
    work(1, around(far - 1)[1])
    work(1, last)
    leaf(1)
    turn_round(1)

    def pass_on(way, turn, batch):
        dest = chip_at(pos + sign[way] * (far - turn))
        sum_copy(batch, dest).wait_recv()
        rs_copy(way, turn - 1, batch, dest).wait_recv()
        partial[batch, dest, core] = (
            gather_sum(batch, dest) + ringbuf[way, turn - 1, batch].astype(jnp.float32)
        ).astype(jnp.bfloat16)
        rs_copy(way, turn, batch, dest).start()

    pass_on(1, 2, 0)
    pass_on(0, 1, 0)
    work(*second(2 * (far - 2)))
    work(1, around(far - 1)[0])
    pass_on(0, 2, 1)
    pass_on(1, 1, 1)

    @pl.loop(2, far - 2)
    def _(turn):
        pass_on(1, turn + 1, 0)
        pass_on(0, turn, 0)
        pass_on(0, turn + 1, 1)
        pass_on(1, turn, 1)

    def pass_half(way, late, half):
        dest = chip_at(pos + sign[way] * (2 - late))
        some = halves[half]
        if late:
            half_copy(way, 0, half, dest).wait_recv()
        partial[way, dest, core, some] = (
            partial[way, dest, core, some].astype(jnp.float32)
            + pairbuf[way, dest, some].astype(jnp.float32)
            + ringbuf[way, far - 3 + late, way, some].astype(jnp.float32)
        ).astype(jnp.bfloat16)
        half_copy(way, late, half, dest).start()

    def pass_late(way):
        dest = chip_at(pos + sign[way] * 2)
        sum_copy(way, dest).wait_recv()
        rs_copy(way, far - 3, way, dest).wait_recv()
        for half in range(2):
            pass_half(way, 0, half)

    pass_on(1, far - 1, 0)
    pass_late(0)
    pass_on(0, far - 1, 1)
    pass_late(1)
    for way in range(2):
        sum_copy(way, chip_at(pos + sign[way])).wait_recv()

    for half in range(2):
        for way in range(2):
            pass_half(way, 1, half)

    shared().wait_send()
    for batch in range(batches):
        exchanged(batch, 0, devices - 1).wait_send()
    some = gathered.at[0, pl.ds(0, chips - 1)]
    remote(some, some, ag_send, sh_recv, partner).wait_send()
    remote(gathered.at[0], gathered.at[0], agp_send, sh_recv, partner).wait_send()
    remote(partial.at[0], partial.at[0], rsp_send, sh_recv, partner).wait_send()

    for batch in range(batches):
        sum_copy(batch, mine).wait_recv()
        rs_copy(1 - batch, far - 1, batch, mine).wait_recv()
        stream[batch] = (
            stream[batch]
            + gather_sum(batch, mine)
            + ringbuf[1 - batch, far - 1, batch].astype(jnp.float32)
        )
    for half in range(2):
        some = halves[half]
        for batch in range(batches):
            half_copy(batch, 1, half, mine).wait_recv()
            out_ref[batch, some] = (
                stream[batch, some] + ringbuf[batch, far - 1, batch, some].astype(jnp.float32)
            ).astype(out_ref.dtype)
    some = partial.at[0, pl.ds(0, chips - 1)]
    remote(some, some, rs_send, sh_recv, partner).wait_send()


def fits(devices, rows, width, hidden):
    block = 2 * rows * (width + 128) * 2
    needed = 3 * devices * block + 3 * width * hidden * 2 + 8 * rows * width * 4
    return devices % 4 == 0 and devices == 2 * 8 and rows % 32 == 0 and 2 * rows % 128 == 0 and needed < 48 * 1024 * 1024


def routed_layer(queries, keys_values, residual, norm_gain, ids, gates, gate_up, down_proj, kv_heads, devices):
    batches, rows, width = residual.shape
    length, part = queries.shape[1:]
    span = length // devices
    hidden = down_proj.shape[1]
    chips = devices // 2
    far = chips // 2
    dma = pltpu.SemaphoreType.DMA
    vmem = pl.BlockSpec(memory_space=pltpu.VMEM)
    anywhere = pl.BlockSpec(memory_space=pl.ANY)
    kind = jnp.bfloat16
    return pl.pallas_call(
        functools.partial(moe_kernel, chips),
        out_shape=pltpu.VMEM((batches, rows, width), kind),
        in_specs=[anywhere] * 8,
        out_specs=vmem,
        scratch_shapes=[
            pltpu.VMEM(queries.shape, kind),
            pltpu.VMEM(keys_values.shape, kind),
            pltpu.VMEM(residual.shape, kind),
            pltpu.VMEM((1, width), jnp.float32),
            pltpu.VMEM((batches, ids.shape[2], rows), jnp.int32),
            pltpu.VMEM((batches, ids.shape[2], rows), jnp.int32),
            pltpu.VMEM((batches, devices, span, part), kind),
            pltpu.VMEM((batches, devices, span, part), kind),
            pltpu.VMEM((batches, rows, width), jnp.float32),
            pltpu.VMEM((batches, chips, 2, rows, width), kind),
            pltpu.VMEM((batches, chips, 2, rows, width), kind),
            pltpu.VMEM((batches, chips, rows, width), kind),
            pltpu.VMEM((2, far, batches, rows, width), kind),
            pltpu.VMEM((width, 2 * hidden), kind),
            pltpu.VMEM((hidden, width), kind),
            pltpu.VMEM((4 * rows, width), kind),
            pltpu.VMEM((4 * rows, batches * rows), jnp.float32),
            pltpu.VMEM((4 * rows, hidden), kind),
            pltpu.VMEM((devices, 1, batches * rows), jnp.float32),
            pltpu.VMEM((devices, 1, batches * rows), jnp.float32),
            dma((2 * batches + 6,)),
            dma, dma,
            dma((batches,)), dma((batches, 2)),
            dma, dma((2, far, batches, 2)),
            dma, dma((batches, chips)),
            dma, dma((batches, chips)),
            dma, dma((2, far, batches)),
            dma((2, 2, 2)),
        ],
        compiler_params=pltpu.CompilerParams(
            collective_id=0, has_side_effects=True, vmem_limit_bytes=56 * 1024 * 1024
        ),
    )(
        queries, keys_values, residual, norm_gain.reshape(1, width),
        jnp.transpose(ids, (0, 2, 1)), jnp.transpose(gates, (0, 2, 1)), gate_up, down_proj,
    )


def body(queries, keys_values, residual, norm_gain, gate_up, down_proj, expert_ids, expert_gates):
    devices = lax.axis_size("dev")
    me = lax.axis_index("dev")
    model_width = residual.shape[2]
    kv_heads = model_width // queries.shape[3]
    experts = devices * gate_up.shape[0]
    batches, unit, length, feat_width = queries.shape
    positions = length // devices
    if batches == 2 and fits(devices, residual.shape[1], model_width, down_proj.shape[1]):
        return routed_layer(
            queries[:, 0], keys_values[:, 0], residual, norm_gain, expert_ids, expert_gates,
            gate_up, down_proj, kv_heads, devices,
        )
    weights = dense_shares(expert_ids, expert_gates, experts)
    blended = attend_local(queries, keys_values)
    weights = lax.all_gather(weights, "dev", axis=1, tiled=True)
    mine = jnp.sum(
        jnp.where(jnp.arange(experts, dtype=jnp.int32) == me, weights, 0.0), axis=-1, keepdims=True
    )
    pieces = []
    for batch_index in range(batches):
        outgoing_rows = blended[batch_index].reshape(1, devices, positions, feat_width)
        arrived_rows = lax.all_to_all(outgoing_rows, "dev", split_axis=1, concat_axis=1, tiled=True)
        attn_rows = to_owners(arrived_rows, kv_heads)
        stream, normed = prepare(attn_rows[0], residual[batch_index], norm_gain)
        rows_in = lax.all_gather(normed, "dev", axis=0, tiled=True)
        partial = run_expert(rows_in, gate_up, down_proj, mine[batch_index])
        summed = lax.psum_scatter(partial, "dev", scatter_dimension=0, tiled=True)
        pieces.append((stream + summed.astype(jnp.float32)).astype(jnp.bfloat16))
    return jnp.stack(pieces, axis=0)


def solution(mesh):
    in_specs = (
        P(None, ("groups", "dev"), None, None),
        P(None, ("groups", "dev"), None, None, None),
        P(None, ("groups", "dev"), None),
        P(),
        P("dev", None, None),
        P("dev", None, None),
        P(None, ("groups", "dev"), None),
        P(None, ("groups", "dev"), None),
    )
    out_specs = P(None, ("groups", "dev"), None)
    return jax.shard_map(body, mesh=mesh, in_specs=in_specs, out_specs=out_specs, check_vma=False)
```
